128 devices in a mesh: seg: 16 (over x, y), head: 8 (over z, core).
Axes of the slice: x: 4, y: 4, z: 4, core: 2. Of those that a mesh axis runs over, the one named last changes fastest.
Arguments:
- query_feat: float32 [1792, 51200], P('head', 'seg'), may hold values from -6 to 6
- key_feat: float32 [1792, 51200], P('head', 'seg'), may hold values from -6 to 6
- value_feat: float32 [1792, 51200], P('head', 'seg'), may hold values from -5.5 to 5.5
- grad_out: float32 [1792, 51200], P('head', 'seg'), may hold values from -6 to 6
- spatial_weight: float32 [3, 3, 1792], replicated, may hold values from -2 to 2
- temporal_weight: float32 [3, 1792], replicated, may hold values from -3.5 to 3.5
Outputs:
- grad_query: float32 [1792, 51200], P('head', 'seg')
- grad_key: float32 [1792, 51200], P('head', 'seg')
- grad_value: float32 [1792, 51200], P('head', 'seg')
- mixed: float32 [64, 20, 40, 1792], P('seg', None, 'head')
The draws below stay inside these ranges and needn't reach their ends.
All inputs are finite; a program needn't handle non-finite values.
Results may differ from the reference program's by a relative error of at most 0.00008.
Values sent between devices are 32-bit elements; how exact they have to be, the bound alone decides.
A program may use at most 128 MiB of HBM per device.

```python
import jax
import jax.numpy as jnp
from jax import lax

HEAD_SIZE = 112
HEADS = 16
ROWS = 20
COLS = 40
FRAMES = 64
TOKENS = 51200
CHANNELS = 1792


def shared_base(key):
    shape = (HEADS * HEAD_SIZE, FRAMES * ROWS * COLS)
    base = jax.random.normal(jax.random.fold_in(key, 101), shape, jnp.float32)
    noise = jax.random.normal(jax.random.fold_in(key, 102), shape, jnp.float32)
    return (jnp.clip(base, -4.0, 4.0), jnp.clip(noise, -3.0, 3.0))


def draw_key_feat(key, part):
    base, noise = shared_base(key)
    return 1.5 * base


def draw_value_feat(key, part):
    base, noise = shared_base(key)
    return base + 0.5 * noise


def levels(rng, dims, pieces, least, high):
    def one(dim, parts):
        heights = jax.random.uniform(jax.random.fold_in(jax.random.fold_in(rng, 6), dim), (parts,), jnp.float32, least / len(pieces), high / len(pieces))
        return jnp.repeat(jnp.exp(heights), dims[dim] // parts).reshape((-1,) + (1,) * (len(dims) - dim - 1))

    factor_of = one(*pieces[0])
    for cut in pieces[1:]:
        factor_of = factor_of * one(*cut)
    return factor_of


def bell_draw(stream_key, shape, deviation, bound, split=(), dtype=jnp.bfloat16):
    drawn = deviation * jax.random.normal(stream_key, shape, jnp.float32)
    if split:
        drawn = drawn * levels(stream_key, shape, split, -0.22, 0.18)
    return jnp.clip(drawn, -bound, bound).astype(dtype)


def setup_inputs(seed: int = 0) -> dict:
    arg_keys = jax.random.split(jax.random.key(seed), 7)
    query_feat = bell_draw(arg_keys[0], (CHANNELS, TOKENS), 1.5, 6.0, ((0, 8), (1, 16)), jnp.float32)
    key_feat = draw_key_feat(jax.random.fold_in(arg_keys[6], 71), 0)
    value_feat = draw_value_feat(jax.random.fold_in(arg_keys[6], 71), 0)
    grad_out = bell_draw(arg_keys[3], (CHANNELS, TOKENS), 1.0, 6.0, ((0, 8), (1, 16)), jnp.float32)
    spatial_weight = bell_draw(arg_keys[4], (3, 3, CHANNELS), 9 ** -0.5, 2.0, (), jnp.float32)
    temporal_weight = bell_draw(arg_keys[5], (3, CHANNELS), 3 ** -0.5, 3.5, (), jnp.float32)
    return dict(query_feat=query_feat, key_feat=key_feat, value_feat=value_feat, grad_out=grad_out, spatial_weight=spatial_weight, temporal_weight=temporal_weight)


exact = lax.Precision.HIGHEST


def head_pass(inputs):
    query_h, key_h, value_h, grad_h = inputs
    feat_query = jnp.exp(query_h)
    feat_key = jnp.exp(key_h)
    local_kv = jnp.einsum('fpd,fpe->fde', feat_key, value_h, precision=exact)
    states = jnp.cumsum(local_kv, axis=0)
    key_sums = jnp.cumsum(jnp.sum(feat_key, axis=1), axis=0)
    numer = jnp.einsum('fpd,fde->fpe', feat_query, states, precision=exact)
    denom = jnp.einsum('fpd,fd->fp', feat_query, key_sums, precision=exact)
    attended = numer / denom[..., None]
    grad_numer = grad_h / denom[..., None]
    grad_denom = -jnp.sum(grad_h * attended, axis=-1) / denom
    grad_query = (jnp.einsum('fpe,fde->fpd', grad_numer, states, precision=exact) + grad_denom[..., None] * key_sums[:, None, :]) * feat_query
    grad_states = jnp.einsum('fpd,fpe->fde', feat_query, grad_numer, precision=exact)
    grad_sums = jnp.einsum('fpd,fp->fd', feat_query, grad_denom, precision=exact)
    later_states = jnp.flip(jnp.cumsum(jnp.flip(grad_states, 0), axis=0), 0)
    later_sums = jnp.flip(jnp.cumsum(jnp.flip(grad_sums, 0), axis=0), 0)
    grad_key = (jnp.einsum('fpe,fde->fpd', value_h, later_states, precision=exact) + later_sums[:, None, :]) * feat_key
    grad_value = jnp.einsum('fpd,fde->fpe', feat_key, later_states, precision=exact)
    return attended, grad_query, grad_key, grad_value


def to_heads(array):
    return jnp.transpose(array.reshape(HEADS, HEAD_SIZE, FRAMES, ROWS * COLS), (0, 2, 3, 1))


def from_heads(array):
    return jnp.transpose(array, (0, 3, 1, 2)).reshape(HEADS * HEAD_SIZE, FRAMES * ROWS * COLS)


def reference(query_feat, key_feat, value_feat, grad_out, spatial_weight, temporal_weight):
    results = lax.map(head_pass, (to_heads(query_feat), to_heads(key_feat), to_heads(value_feat), to_heads(grad_out)))
    attended_heads, grad_query, grad_key, grad_value = results
    attended = jnp.moveaxis(attended_heads, 0, 2).reshape(FRAMES, ROWS, COLS, HEADS * HEAD_SIZE)
    padded = jnp.pad(attended, ((0, 0), (1, 1), (1, 1), (0, 0)))
    spatial = jnp.zeros_like(attended)
    for row_off in range(3):
        for col_off in range(3):
            spatial = spatial + spatial_weight[row_off, col_off] * padded[:, row_off:row_off + ROWS, col_off:col_off + COLS]
    active = jax.nn.silu(spatial)
    past = jnp.pad(active, ((2, 0), (0, 0), (0, 0), (0, 0)))
    mixed = jnp.zeros_like(active)
    for lag in range(3):
        mixed = mixed + temporal_weight[lag] * past[2 - lag:2 - lag + FRAMES]
    return from_heads(grad_query), from_heads(grad_key), from_heads(grad_value), mixed
```

```python
import functools

import jax
import jax.numpy as jnp
from jax import lax
from jax.experimental import pallas as pl
from jax.experimental.pallas import tpu as pltpu
from jax.sharding import PartitionSpec as P

D = 112
ROWS = 20
COLS = 40
FRAMES = 4
STRIDE = 768
WIN = 896
HEADS = 2
STRIPS = 8
CELLS = 100
CHUNKS = ((0, 256), (256, 256), (512, 256), (768, 128))
BASE = 136
MESH = pl.DeviceIdType.MESH
F32 = jnp.float32
BF16 = jnp.bfloat16
VMEM_LIMIT = 60 * 1024 * 1024


def split(x):
    hi = x.astype(BF16)
    lo = (x - hi.astype(F32)).astype(BF16)
    return hi, lo


def nn(a, b):
    return lax.dot_general(a, b, (((1,), (0,)), ((), ())), preferred_element_type=F32)


def nt(a, b):
    return lax.dot_general(a, b, (((1,), (1,)), ((), ())), preferred_element_type=F32)


def pad_rows(x):
    return jnp.concatenate([x, jnp.zeros((16, x.shape[1]), x.dtype)], axis=0)


def left_mul(pair, b_hi, b_lo):
    return nn(pair, jnp.concatenate([b_hi, b_hi], axis=0)) + nn(pair[:, :128], b_lo)


def outer(a_hi, a_lo, b_hi, b_lo):
    both = nt(jnp.concatenate([a_hi, a_lo], axis=0), b_hi)
    rows = a_hi.shape[0]
    return both[:rows] + both[rows:] + nt(a_hi, b_lo)


def in_frame(frame, start, width):
    lane = lax.broadcasted_iota(jnp.int32, (1, width), 1) + start
    return (lane >= 32 * frame) & (lane < 32 * frame + ROWS * COLS)


def extra_row(row):
    place = lax.broadcasted_iota(jnp.int32, (16, row.shape[1]), 0)
    return jnp.where(place == 0, jnp.broadcast_to(row, (16, row.shape[1])), 0.0)


def side_by_side(x):
    hi, lo = split(x)
    return jnp.concatenate([hi, lo], axis=1)


def sums_kernel(k_ref, v_ref, out_ref, k_win, v_win, sem):
    def copies(h, f):
        rows = pl.ds(D * h, D)
        lanes = pl.ds(STRIDE * f, WIN)
        return (
            pltpu.make_async_copy(k_ref.at[rows, lanes], k_win.at[h, f], sem.at[0, h, f]),
            pltpu.make_async_copy(v_ref.at[rows, lanes], v_win.at[h, f], sem.at[1, h, f]),
        )

    for h in range(HEADS):
        for f in range(FRAMES):
            for c in copies(h, f):
                c.start()
    for h in range(HEADS):
        def one(f, total, h=h):
            for c in copies(h, f):
                c.wait()
            for start, width in CHUNKS:
                lanes = slice(start, start + width)
                ok = in_frame(f, start, width)
                k_hi, k_lo = split(jnp.where(ok, jnp.exp(k_win[h, f, :, lanes]), 0.0))
                v_hi, v_lo = split(v_win[h, f, :, lanes])
                ones = extra_row(jnp.ones((1, width), F32)).astype(BF16)
                v_hi = jnp.concatenate([v_hi, ones], axis=0)
                total = total + outer(k_hi, k_lo, v_hi, pad_rows(v_lo))
            out_ref[h, f] = total
            return total

        lax.fori_loop(0, FRAMES, one, jnp.zeros((D, 128), F32))


def key_value_sums(key_feat, value_feat):
    return pl.pallas_call(
        sums_kernel,
        out_shape=jax.ShapeDtypeStruct((HEADS, FRAMES, D, 128), F32),
        in_specs=[pl.BlockSpec(memory_space=pl.ANY)] * 2,
        out_specs=pl.BlockSpec(memory_space=pltpu.VMEM),
        scratch_shapes=[
            pltpu.VMEM((HEADS, FRAMES, D, WIN), F32),
            pltpu.VMEM((HEADS, FRAMES, D, WIN), F32),
            pltpu.SemaphoreType.DMA((2, HEADS, FRAMES)),
        ],
        compiler_params=pltpu.CompilerParams(vmem_limit_bytes=VMEM_LIMIT),
        name="key_value_sums",
    )(key_feat, value_feat)


def greet(devices):
    barrier = pltpu.get_barrier_semaphore()
    for dev in devices:
        pl.semaphore_signal(barrier, inc=1, device_id=dev, device_id_type=MESH)
    pl.semaphore_wait(barrier, len(devices))


def scan_peers():
    seg, head = lax.axis_index("seg"), lax.axis_index("head")
    x, y = seg // 4, seg % 4
    along_y = [(x * 4 + (y + k) % 4, head) for k in range(1, 4)]
    along_x = [(((x + k) % 4) * 4 + y, head) for k in range(1, 4)]
    return along_y, along_x


SCAN_SCRATCH = [
    pltpu.VMEM((4, 56, 128), F32),
    pltpu.VMEM((56, 128), F32),
    pltpu.VMEM((4, 56, 128), F32),
    pltpu.VMEM((4, 56, 128), F32),
    pltpu.SemaphoreType.DMA((3, 4)),
    pltpu.SemaphoreType.DMA((3, 4)),
]


class Scan:
    def __init__(self, own, result, scratch, reverse):
        self.own, self.result, self.reverse = own, result, reverse
        self.got, self.line, self.lines, self.back, self.send, self.recv = scratch
        seg = lax.axis_index("seg")
        self.x, self.y = seg // 4, seg % 4
        self.along_y, self.along_x = scan_peers()

    def copy(self, phase, k, src, dst, dev):
        return pltpu.make_async_remote_copy(
            src_ref=src, dst_ref=dst, send_sem=self.send.at[phase, k], recv_sem=self.recv.at[phase, k],
            device_id=dev, device_id_type=MESH,
        )

    def first(self):
        self.c1 = [
            self.copy(0, k, self.own.at[(self.y + k) % 4], self.got.at[k], self.along_y[k - 1])
            for k in range(1, 4)
        ]
        for c in self.c1:
            c.start()

    def second(self):
        for c in self.c1:
            c.wait()
        mine = self.own[self.y]
        self.line[...] = mine + self.got[1] + self.got[2] + self.got[3]
        self.c2 = [
            self.copy(1, k, self.line, self.lines.at[k], self.along_x[k - 1]) for k in range(1, 4)
        ]
        for c in self.c2:
            c.start()

    def counts(self, place, source):
        return source > place if self.reverse else source < place

    def third(self):
        for c in self.c2:
            c.wait()
        zero = jnp.zeros((56, 128), F32)
        before = zero
        for k in range(1, 4):
            source = (self.x + 4 - k) % 4
            before = before + jnp.where(self.counts(self.x, source), self.lines[k], zero)
        terms = [(self.y, self.own[self.y])] + [((self.y + 4 - k) % 4, self.got[k]) for k in range(1, 4)]
        for k in range(4):
            target = (self.y + k) % 4
            total = before
            for source, value in terms:
                total = total + jnp.where(self.counts(target, source), value, zero)
            self.back[k] = total
        self.c3 = [
            self.copy(2, k, self.back.at[k], self.result.at[self.y], self.along_y[k - 1]) for k in range(1, 4)
        ]
        for c in self.c3:
            c.start()
        self.result[self.y] = self.back[0]

    def last(self):
        for c in self.c3:
            c.wait()


def scan_kernel(own_ref, out_ref, result, *scratch):
    along_y, along_x = scan_peers()
    greet(along_y + along_x)
    scan = Scan(own_ref, result, scratch, False)
    scan.first()
    scan.second()
    scan.third()
    scan.last()
    out_ref[...] = result[...]


def prefix(own):
    return pl.pallas_call(
        scan_kernel,
        out_shape=jax.ShapeDtypeStruct((4, 56, 128), F32),
        in_specs=[pl.BlockSpec(memory_space=pltpu.VMEM)],
        out_specs=pl.BlockSpec(memory_space=pltpu.VMEM),
        scratch_shapes=[pltpu.VMEM((4, 56, 128), F32)] + SCAN_SCRATCH,
        compiler_params=pltpu.CompilerParams(collective_id=0, has_side_effects=True),
        name="prefix",
    )(own)


def state_of(before_ref, local_ref, h, f):
    return before_ref[h] + local_ref[h, f]


def query_frame(f, q_win, g_win, before_ref, local_ref, gq_ref, ds_ref, att, conv_in, w_ref, send_ref):
    for h in range(HEADS):
        state = state_of(before_ref, local_ref, h, f)
        plain = side_by_side(state)
        turned = side_by_side(pad_rows(state).T)
        rows = slice(D * h, D * h + D)
        grad_state = jnp.zeros((D, 128), F32)
        for start, width in CHUNKS:
            lanes = slice(start, start + width)
            ok = in_frame(f, start, width)
            feat = jnp.exp(q_win[f, rows, lanes])
            q_hi, q_lo = split(feat)
            numer = left_mul(turned, pad_rows(q_hi), pad_rows(q_lo))
            inverse = 1.0 / numer[D:D + 1]
            attended = numer[:D] * inverse
            att[rows, lanes] = jnp.where(ok, attended, 0.0)
            grad = g_win[f, rows, lanes]
            slope = -jnp.sum(grad * attended, axis=0, keepdims=True) * inverse
            ext = jnp.where(ok, jnp.concatenate([grad * inverse, extra_row(slope)], axis=0), 0.0)
            n_hi, n_lo = split(ext)
            gq = left_mul(plain, n_hi, n_lo) * feat
            place = pl.ds(pl.multiple_of(STRIDE * f + start, 128), width)
            gq_ref[rows, place] = jnp.where(ok, gq, gq_ref[rows, place])
            grad_state = grad_state + outer(q_hi, q_lo, n_hi, n_lo)
        ds_ref[h, f] = grad_state
    for m in range(WIN // 128):
        place = pl.ds(pl.multiple_of(BASE - 32 * f + 128 * m, 8), 128)
        conv_in[place, :] = att[:, 128 * m:128 * m + 128].T
    edge = lax.broadcasted_iota(jnp.int32, (COLS, 128), 0)
    for lane in range(2):
        lanes = slice(128 * lane, 128 * lane + 128)
        taps = [[w_ref[3 * i + j:3 * i + j + 1, lanes] for j in range(3)] for i in range(3)]
        for r in range(ROWS):
            lines = [conv_in[BASE + COLS * (r + i - 1):BASE + COLS * (r + i), lanes] for i in range(3)]
            cols = [taps[0][j] * lines[0] + taps[1][j] * lines[1] + taps[2][j] * lines[2] for j in range(3)]
            total = (
                cols[1]
                + jnp.where(edge == 0, 0.0, pltpu.roll(cols[0], 1, 0))
                + jnp.where(edge == COLS - 1, 0.0, pltpu.roll(cols[2], COLS - 1, 0))
            )
            half = 0.5 * total
            act = half + half * jnp.tanh(half)
            for j in range(STRIPS):
                send_ref[f, j, 5 * r:5 * r + 5, lanes] = act[5 * j:5 * j + 5]


def query_kernel(q_ref, g_ref, before_ref, local_ref, w_ref, gq_ref, ds_ref, send_ref, q_win, g_win, att, conv_in, sem):
    def copies(f):
        lanes = pl.ds(STRIDE * f, WIN)
        return (
            pltpu.make_async_copy(q_ref.at[:, lanes], q_win.at[f], sem.at[0, f]),
            pltpu.make_async_copy(g_ref.at[:, lanes], g_win.at[f], sem.at[1, f]),
        )

    for f in range(FRAMES):
        for c in copies(f):
            c.start()
    att[...] = jnp.zeros_like(att)
    conv_in[...] = jnp.zeros_like(conv_in)

    def one(f, carry):
        for c in copies(f):
            c.wait()
        query_frame(f, q_win, g_win, before_ref, local_ref, gq_ref, ds_ref, att, conv_in, w_ref, send_ref)
        return carry

    lax.fori_loop(0, FRAMES, one, 0)
    for h in range(HEADS):
        for f in range(FRAMES - 2, -1, -1):
            ds_ref[h, f] = ds_ref[h, f] + ds_ref[h, f + 1]


def query_side(q, g, before, local, weights):
    vmem = pl.BlockSpec(memory_space=pltpu.VMEM)
    return pl.pallas_call(
        query_kernel,
        out_shape=(
            jax.ShapeDtypeStruct((HEADS * D, STRIDE * 3 + WIN), F32),
            jax.ShapeDtypeStruct((HEADS, FRAMES, D, 128), F32),
            jax.ShapeDtypeStruct((FRAMES, STRIPS, CELLS, 256), F32),
        ),
        in_specs=[pl.BlockSpec(memory_space=pl.ANY)] * 2 + [vmem] * 3,
        out_specs=(vmem, vmem, vmem),
        scratch_shapes=[
            pltpu.VMEM((FRAMES, HEADS * D, WIN), F32),
            pltpu.VMEM((FRAMES, HEADS * D, WIN), F32),
            pltpu.VMEM((256, WIN), F32),
            pltpu.VMEM((BASE + WIN, 256), F32),
            pltpu.SemaphoreType.DMA((2, FRAMES)),
        ],
        compiler_params=pltpu.CompilerParams(vmem_limit_bytes=VMEM_LIMIT),
        name="query_side",
    )(q, g, before, local, weights)


ORDER = (2, 3, 0, 1)
HOPS = (1, 2, 6, 3, 5, 7, 4)


def exchange_kernel(act_ref, own_ref, got_ref, halo_ref, after_ref, result, send, recv, fsend, frecv, lsem, *scratch):
    seg, head = lax.axis_index("seg"), lax.axis_index("head")
    along_y, along_x = scan_peers()
    peers = [(seg, head ^ k) for k in range(1, 8)]
    up, down = ((seg + 1) % 16, head), ((seg + 15) % 16, head)
    barrier = pltpu.get_barrier_semaphore()
    for dev in along_y + along_x + peers + [up, down]:
        pl.semaphore_signal(barrier, inc=1, device_id=dev, device_id_type=MESH)
    pl.semaphore_wait(barrier, 15)

    def strip(f, k):
        return pltpu.make_async_remote_copy(
            src_ref=act_ref.at[f, head ^ k], dst_ref=got_ref.at[k, f], send_sem=send.at[f, k], recv_sem=recv.at[f, k],
            device_id=(seg, head ^ k), device_id_type=MESH,
        )

    def forward(f, k):
        src = act_ref.at[f, head] if k == 0 else got_ref.at[k, f]
        return pltpu.make_async_remote_copy(
            src_ref=src, dst_ref=halo_ref.at[k, f - 2], send_sem=fsend.at[f - 2, k], recv_sem=frecv.at[f - 2, k],
            device_id=up, device_id_type=MESH,
        )

    scan = Scan(own_ref, result, scratch, True)
    scan.first()
    for f in ORDER:
        for k in HOPS:
            strip(f, k).start()
    for f in (2, 3):
        forward(f, 0).start()
    for f in range(FRAMES):
        pltpu.make_async_copy(act_ref.at[f, head], got_ref.at[0, f], lsem.at[f]).start()
    scan.second()
    scan.third()
    scan.last()
    after_ref[...] = result[...]
    for f in (2, 3):
        for k in HOPS:
            strip(f, k).wait_recv()
            forward(f, k).start()
    for f in range(FRAMES):
        pltpu.make_async_copy(act_ref.at[f, head], got_ref.at[0, f], lsem.at[f]).wait()
    for f in (0, 1):
        for k in HOPS:
            strip(f, k).wait_recv()
    for f in ORDER:
        for k in HOPS:
            strip(f, k).wait_send()
    for f in (2, 3):
        for k in (0,) + HOPS:
            forward(f, k).wait()


def exchange(act, own):
    hbm = pl.BlockSpec(memory_space=pl.ANY)
    vmem = pl.BlockSpec(memory_space=pltpu.VMEM)
    return pl.pallas_call(
        exchange_kernel,
        out_shape=(
            jax.ShapeDtypeStruct((STRIPS, FRAMES, CELLS, 256), F32),
            jax.ShapeDtypeStruct((STRIPS, 2, CELLS, 256), F32),
            jax.ShapeDtypeStruct((4, 56, 128), F32),
        ),
        in_specs=[hbm, vmem],
        out_specs=(hbm, hbm, vmem),
        scratch_shapes=[
            pltpu.VMEM((4, 56, 128), F32),
            pltpu.SemaphoreType.DMA((FRAMES, 8)),
            pltpu.SemaphoreType.DMA((FRAMES, 8)),
            pltpu.SemaphoreType.DMA((2, 8)),
            pltpu.SemaphoreType.DMA((2, 8)),
            pltpu.SemaphoreType.DMA((FRAMES,)),
        ] + SCAN_SCRATCH,
        compiler_params=pltpu.CompilerParams(collective_id=1, has_side_effects=True, vmem_limit_bytes=8 << 20),
        name="exchange",
    )(act, own)


def mix_group(base, count, halo_on, got, halo, tw_ref, tmp, mixed_ref):
    head = lax.axis_index("head")
    place = lax.broadcasted_iota(jnp.int32, (count, 128), 1)
    pending = [None] * FRAMES
    for owner in range(STRIPS):
        slot = head ^ owner
        for lane in range(2):
            lanes = slice(128 * lane, 128 * lane + 128)
            acts = [jnp.where(halo_on, halo[slot, i, pl.ds(base, count), lanes], 0.0) for i in range(2)]
            acts += [got[slot, f, pl.ds(base, count), lanes] for f in range(FRAMES)]
            w = [tw_ref[owner, i:i + 1, lanes] for i in range(3)]
            width = 128 if lane == 0 else 96
            tile, shift = divmod(224 * owner + 128 * lane, 128)
            for f in range(FRAMES):
                val = w[0] * acts[f + 2] + w[1] * acts[f + 1] + w[2] * acts[f]
                full = val
                if shift:
                    val = pltpu.roll(val, shift, 1)
                    full = jnp.where(place < shift, pending[f], val)
                if shift + width >= 128:
                    tmp[tile, pl.ds(f, count, stride=4), :] = full
                    pending[f] = val
                else:
                    pending[f] = full


def key_kernel(k_ref, v_ref, after_ref, local_ref, got_hbm, halo_hbm, tw_ref, gk_ref, gv_ref, mixed_ref,
               k_win, v_win, got, halo, tmp, sem, sem2):
    def copies(f):
        lanes = pl.ds(STRIDE * f, WIN)
        return (
            pltpu.make_async_copy(k_ref.at[:, lanes], k_win.at[f], sem.at[0, f]),
            pltpu.make_async_copy(v_ref.at[:, lanes], v_win.at[f], sem.at[1, f]),
        )

    for f in range(FRAMES):
        for c in copies(f):
            c.start()
    got_copy = pltpu.make_async_copy(got_hbm, got, sem2.at[0])
    halo_copy = pltpu.make_async_copy(halo_hbm, halo, sem2.at[1])
    got_copy.start()
    halo_copy.start()

    def one(f, carry):
        for c in copies(f):
            c.wait()
        for h in range(HEADS):
            state = state_of(after_ref, local_ref, h, f)
            plain = side_by_side(state)
            turned = side_by_side(pad_rows(state).T)
            rows = slice(D * h, D * h + D)
            for start, width in CHUNKS:
                lanes = slice(start, start + width)
                ok = in_frame(f, start, width)
                feat = jnp.exp(k_win[f, rows, lanes])
                k_hi, k_lo = split(feat)
                v_hi, v_lo = split(v_win[f, rows, lanes])
                ones = extra_row(jnp.ones((1, width), F32)).astype(BF16)
                v_hi = jnp.concatenate([v_hi, ones], axis=0)
                gk = left_mul(plain, v_hi, pad_rows(v_lo)) * feat
                gv = left_mul(turned, pad_rows(k_hi), pad_rows(k_lo))[:D]
                place = pl.ds(pl.multiple_of(STRIDE * f + start, 128), width)
                gk_ref[rows, place] = jnp.where(ok, gk, gk_ref[rows, place])
                gv_ref[rows, place] = jnp.where(ok, gv, gv_ref[rows, place])
        return carry

    lax.fori_loop(0, FRAMES, one, 0)
    got_copy.wait()
    halo_copy.wait()
    halo_on = lax.axis_index("seg") > 0

    def group(base, count):
        mix_group(base, count, halo_on, got, halo, tw_ref, tmp, mixed_ref)
        for i in range(count):
            for t in range(14):
                mixed_ref[base + i, :, 128 * t:128 * t + 128] = tmp[t, 4 * i:4 * i + 4, :]

    def step(i, carry):
        group(pl.multiple_of(8 * i, 8), 8)
        return carry

    lax.fori_loop(0, 12, step, 0)
    group(96, 4)


def key_side(k, v, after, local, got, halo, tw):
    vmem = pl.BlockSpec(memory_space=pltpu.VMEM)
    hbm = pl.BlockSpec(memory_space=pl.ANY)
    return pl.pallas_call(
        key_kernel,
        out_shape=(
            jax.ShapeDtypeStruct((HEADS * D, 3200), F32),
            jax.ShapeDtypeStruct((HEADS * D, 3200), F32),
            jax.ShapeDtypeStruct((CELLS, FRAMES, 1792), F32),
        ),
        in_specs=[hbm, hbm, vmem, vmem, hbm, hbm, vmem],
        out_specs=(vmem, vmem, vmem),
        scratch_shapes=[
            pltpu.VMEM((FRAMES, HEADS * D, WIN), F32),
            pltpu.VMEM((FRAMES, HEADS * D, WIN), F32),
            pltpu.VMEM((STRIPS, FRAMES, CELLS, 256), F32),
            pltpu.VMEM((STRIPS, 2, CELLS, 256), F32),
            pltpu.VMEM((14, 32, 128), F32),
            pltpu.SemaphoreType.DMA((2, FRAMES)),
            pltpu.SemaphoreType.DMA((2,)),
        ],
        compiler_params=pltpu.CompilerParams(vmem_limit_bytes=VMEM_LIMIT),
        name="key_side",
    )(k, v, after, local, got, halo, tw)


def body(query_feat, key_feat, value_feat, grad_out, spatial_weight, temporal_weight):
    head = lax.axis_index("head")
    chans = HEADS * D
    w_own = lax.dynamic_slice_in_dim(spatial_weight.reshape(9, STRIPS * chans), head * chans, chans, axis=1)
    w_own = jnp.pad(w_own, ((0, 0), (0, 256 - chans)))
    tw = jnp.pad(jnp.transpose(temporal_weight.reshape(3, STRIPS, chans), (1, 0, 2)), ((0, 0), (0, 0), (0, 256 - chans)))
    local = key_value_sums(key_feat, value_feat)
    before = prefix(local[:, FRAMES - 1].reshape(4, 56, 128)).reshape(HEADS, D, 128)
    gq, later, act = query_side(query_feat, grad_out, before, local, w_own)
    got, halo, after = exchange(act, later[:, 0].reshape(4, 56, 128))
    gk, gv, mixed = key_side(key_feat, value_feat, after.reshape(HEADS, D, 128), later, got, halo, tw)
    mixed = jnp.transpose(mixed.reshape(ROWS, 5, FRAMES, STRIPS * chans), (2, 0, 1, 3))
    return gq, gk, gv, mixed


def solution(mesh):
    wide = P("head", "seg")
    in_specs = (wide, wide, wide, wide, P(), P())
    out_specs = (wide, wide, wide, P("seg", None, "head", None))
    return jax.shard_map(body, mesh=mesh, in_specs=in_specs, out_specs=out_specs, check_vma=False)
```

```python
import functools

import jax
import jax.numpy as jnp
from jax import lax
from jax.experimental import pallas as pl
from jax.experimental.pallas import tpu as pltpu
from jax.sharding import PartitionSpec as P

D = 112
ROWS = 20
COLS = 40
FRAMES = 4
STRIDE = 768
WIN = 896
HEADS = 2
STRIPS = 8
CELLS = 100
CHUNKS = ((0, 256), (256, 256), (512, 256), (768, 128))
BASE = 136
MESH = pl.DeviceIdType.MESH
F32 = jnp.float32
BF16 = jnp.bfloat16
VMEM_LIMIT = 60 * 1024 * 1024


def split(x):
    hi = x.astype(BF16)
    lo = (x - hi.astype(F32)).astype(BF16)
    return hi, lo


def nn(a, b):
    return lax.dot_general(a, b, (((1,), (0,)), ((), ())), preferred_element_type=F32)


def nt(a, b):
    return lax.dot_general(a, b, (((1,), (1,)), ((), ())), preferred_element_type=F32)


def pad_rows(x):
    return jnp.concatenate([x, jnp.zeros((16, x.shape[1]), x.dtype)], axis=0)


def left_mul(pair, b_hi, b_lo):
    return nn(pair, jnp.concatenate([b_hi, b_hi], axis=0)) + nn(pair[:, :128], b_lo)


def outer(a_hi, a_lo, b_hi, b_lo):
    both = nt(jnp.concatenate([a_hi, a_lo], axis=0), b_hi)
    rows = a_hi.shape[0]
    return both[:rows] + both[rows:] + nt(a_hi, b_lo)


def in_frame(frame, start, width):
    lane = lax.broadcasted_iota(jnp.int32, (1, width), 1) + start
    return (lane >= 32 * frame) & (lane < 32 * frame + ROWS * COLS)


def extra_row(row):
    place = lax.broadcasted_iota(jnp.int32, (16, row.shape[1]), 0)
    return jnp.where(place == 0, jnp.broadcast_to(row, (16, row.shape[1])), 0.0)


def side_by_side(x):
    hi, lo = split(x)
    return jnp.concatenate([hi, lo], axis=1)


def greet(devices):
    barrier = pltpu.get_barrier_semaphore()
    for dev in devices:
        pl.semaphore_signal(barrier, inc=1, device_id=dev, device_id_type=MESH)
    pl.semaphore_wait(barrier, len(devices))


def scan_peers():
    seg, head = lax.axis_index("seg"), lax.axis_index("head")
    x, y = seg // 4, seg % 4
    along_y = [(x * 4 + (y + k) % 4, head) for k in range(1, 4)]
    along_x = [(((x + k) % 4) * 4 + y, head) for k in range(1, 4)]
    return along_y, along_x


SCAN_SCRATCH = [
    pltpu.VMEM((4, 56, 128), F32),
    pltpu.VMEM((56, 128), F32),
    pltpu.VMEM((4, 56, 128), F32),
    pltpu.VMEM((4, 56, 128), F32),
    pltpu.SemaphoreType.DMA((3, 4)),
    pltpu.SemaphoreType.DMA((3, 4)),
]


class Scan:
    def __init__(self, own, result, scratch, reverse):
        self.own, self.result, self.reverse = own, result, reverse
        self.got, self.line, self.lines, self.back, self.send, self.recv = scratch
        seg = lax.axis_index("seg")
        self.x, self.y = seg // 4, seg % 4
        self.along_y, self.along_x = scan_peers()

    def copy(self, phase, k, src, dst, dev):
        return pltpu.make_async_remote_copy(
            src_ref=src, dst_ref=dst, send_sem=self.send.at[phase, k], recv_sem=self.recv.at[phase, k],
            device_id=dev, device_id_type=MESH,
        )

    def first(self):
        self.c1 = [
            self.copy(0, k, self.own.at[(self.y + k) % 4], self.got.at[k], self.along_y[k - 1])
            for k in range(1, 4)
        ]
        for c in self.c1:
            c.start()

    def second(self):
        for c in self.c1:
            c.wait()
        mine = self.own[self.y]
        self.line[...] = mine + self.got[1] + self.got[2] + self.got[3]
        self.c2 = [
            self.copy(1, k, self.line, self.lines.at[k], self.along_x[k - 1]) for k in range(1, 4)
        ]
        for c in self.c2:
            c.start()

    def counts(self, place, source):
        return source > place if self.reverse else source < place

    def third(self):
        for c in self.c2:
            c.wait()
        zero = jnp.zeros((56, 128), F32)
        before = zero
        for k in range(1, 4):
            source = (self.x + 4 - k) % 4
            before = before + jnp.where(self.counts(self.x, source), self.lines[k], zero)
        terms = [(self.y, self.own[self.y])] + [((self.y + 4 - k) % 4, self.got[k]) for k in range(1, 4)]
        for k in range(4):
            target = (self.y + k) % 4
            total = before
            for source, value in terms:
                total = total + jnp.where(self.counts(target, source), value, zero)
            self.back[k] = total
        self.c3 = [
            self.copy(2, k, self.back.at[k], self.result.at[self.y], self.along_y[k - 1]) for k in range(1, 4)
        ]
        for c in self.c3:
            c.start()
        self.result[self.y] = self.back[0]

    def last(self):
        for c in self.c3:
            c.wait()


def ones_row(width):
    return extra_row(jnp.ones((1, width), F32)).astype(BF16)


def sums_frame(h, f, k_win, v_win):
    rows = slice(D * h, D * h + D)
    total = jnp.zeros((D, 128), F32)
    for start, width in CHUNKS:
        lanes = slice(start, start + width)
        ok = in_frame(f, start, width)
        k_hi, k_lo = split(jnp.where(ok, jnp.exp(k_win[f, rows, lanes]), 0.0))
        v_hi, v_lo = split(v_win[f, rows, lanes])
        v_hi = jnp.concatenate([v_hi, ones_row(width)], axis=0)
        total = total + outer(k_hi, k_lo, v_hi, pad_rows(v_lo))
    return total


def rows_of(ref, h):
    return jnp.concatenate([ref[2 * h], ref[2 * h + 1]], axis=0)


def attend(f, q_win, state, att, inv):
    for h in range(HEADS):
        turned = side_by_side(pad_rows(state(h, f)).T)
        rows = slice(D * h, D * h + D)
        for start, width in CHUNKS:
            lanes = slice(start, start + width)
            q_hi, q_lo = split(jnp.exp(q_win[f, rows, lanes]))
            numer = left_mul(turned, pad_rows(q_hi), pad_rows(q_lo))
            inverse = 1.0 / numer[D:D + 1]
            att[f, rows, lanes] = jnp.where(in_frame(f, start, width), numer[:D] * inverse, 0.0)
            inv[f, h, 0:1, lanes] = inverse


def convolve(f, att, conv_in, w_own, send):
    for m in range(WIN // 128):
        place = BASE - 32 * f + 128 * m
        conv_in[place:place + 128, :] = att[f, :, 128 * m:128 * m + 128].T
    edge = lax.broadcasted_iota(jnp.int32, (COLS, 128), 0)
    for lane in range(2):
        lanes = slice(128 * lane, 128 * lane + 128)
        taps = [[w_own[i, j:j + 1, lanes] for j in range(3)] for i in range(3)]
        for r in range(ROWS):
            lines = [conv_in[BASE + COLS * (r + i - 1):BASE + COLS * (r + i), lanes] for i in range(3)]
            cols = [taps[0][j] * lines[0] + taps[1][j] * lines[1] + taps[2][j] * lines[2] for j in range(3)]
            total = (
                cols[1]
                + jnp.where(edge == 0, 0.0, pltpu.roll(cols[0], 1, 0))
                + jnp.where(edge == COLS - 1, 0.0, pltpu.roll(cols[2], COLS - 1, 0))
            )
            half = 0.5 * total
            act = half + half * jnp.tanh(half)
            for j in range(STRIPS):
                send[f, j, 5 * r:5 * r + 5, lanes] = act[5 * j:5 * j + 5]


def place_of(f, start, width):
    return slice(STRIDE * f + start, STRIDE * f + start + width)


def query_grads(f, q_win, g_win, state, att, inv, gq_ref, ds):
    for h in range(HEADS):
        plain = side_by_side(state(h, f))
        rows = slice(D * h, D * h + D)
        grad_state = jnp.zeros((D, 128), F32)
        for start, width in CHUNKS:
            lanes = slice(start, start + width)
            ok = in_frame(f, start, width)
            feat = jnp.exp(q_win[f, rows, lanes])
            q_hi, q_lo = split(feat)
            inverse = inv[f, h, 0:1, lanes]
            grad = g_win[f, rows, lanes]
            slope = -jnp.sum(grad * att[f, rows, lanes], axis=0, keepdims=True) * inverse
            ext = jnp.where(ok, jnp.concatenate([grad * inverse, extra_row(slope)], axis=0), 0.0)
            n_hi, n_lo = split(ext)
            gq = left_mul(plain, n_hi, n_lo) * feat
            place = place_of(f, start, width)
            gq_ref[rows, place] = jnp.where(ok, gq, gq_ref[rows, place])
            grad_state = grad_state + outer(q_hi, q_lo, n_hi, n_lo)
        ds[h, f] = grad_state


def key_grads(f, k_win, v_win, state, gk_ref, gv_ref):
    for h in range(HEADS):
        plain = side_by_side(state(h, f))
        turned = side_by_side(pad_rows(state(h, f)).T)
        rows = slice(D * h, D * h + D)
        for start, width in CHUNKS:
            lanes = slice(start, start + width)
            ok = in_frame(f, start, width)
            feat = jnp.exp(k_win[f, rows, lanes])
            k_hi, k_lo = split(feat)
            v_hi, v_lo = split(v_win[f, rows, lanes])
            v_hi = jnp.concatenate([v_hi, ones_row(width)], axis=0)
            gk = left_mul(plain, v_hi, pad_rows(v_lo)) * feat
            gv = left_mul(turned, pad_rows(k_hi), pad_rows(k_lo))[:D]
            place = place_of(f, start, width)
            gk_ref[rows, place] = jnp.where(ok, gk, gk_ref[rows, place])
            gv_ref[rows, place] = jnp.where(ok, gv, gv_ref[rows, place])


ORDER = (2, 3, 0, 1)
HOPS = (1, 2, 6, 3, 5, 7, 4)


def main_kernel(q_ref, k_ref, v_ref, g_ref, sw_ref, gq_ref, gk_ref, gv_ref, got_ref, halo_ref,
                q_win, k_win, v_win, g_win, att, inv, conv_in, act, w_own, local, ds, own, before, after,
                load, send, recv, fsend, frecv, lsem, *scratch):
    seg, head = lax.axis_index("seg"), lax.axis_index("head")
    along_y, along_x = scan_peers()
    peers = [(seg, head ^ k) for k in range(1, 8)]
    up, down = ((seg + 1) % 16, head), ((seg + 15) % 16, head)
    barrier = pltpu.get_barrier_semaphore()
    for dev in along_y + along_x + peers + [up, down]:
        pl.semaphore_signal(barrier, inc=1, device_id=dev, device_id_type=MESH)

    wins = ((k_ref, k_win), (v_ref, v_win), (q_ref, q_win), (g_ref, g_win))

    def loading(i, f):
        src, dst = wins[i]
        return pltpu.make_async_copy(src.at[:, STRIDE * f:STRIDE * f + WIN], dst.at[f], load.at[i, f])

    for f in range(FRAMES):
        for i in range(2):
            loading(i, f).start()
    for i in (2, 3):
        for f in ORDER:
            loading(i, f).start()

    def strip(f, k):
        return pltpu.make_async_remote_copy(
            src_ref=act.at[f, head ^ k], dst_ref=got_ref.at[k, f], send_sem=send.at[f, k], recv_sem=recv.at[f, k],
            device_id=(seg, head ^ k), device_id_type=MESH,
        )

    def forward(f, k):
        src = act.at[f, head] if k == 0 else got_ref.at[k, f]
        return pltpu.make_async_remote_copy(
            src_ref=src, dst_ref=halo_ref.at[k, f - 2], send_sem=fsend.at[f - 2, k], recv_sem=frecv.at[f - 2, k],
            device_id=up, device_id_type=MESH,
        )

    def mine(f):
        return pltpu.make_async_copy(act.at[f, head], got_ref.at[0, f], lsem.at[f])

    queue = [(2, 0), (3, 0), (2, 1), (3, 1)] + [(2, k) for k in HOPS[1:]] + [(3, k) for k in HOPS[1:]]

    def pass_on(count):
        for f, k in queue[:count]:
            if k:
                strip(f, k).wait_recv()
            forward(f, k).start()
        del queue[:count]

    lanes = pl.ds(0, 256)
    chans = HEADS * D
    for i in range(3):
        taps = sw_ref[i, :, :256]
        for o in range(1, STRIPS):
            begin = min(chans * o, STRIPS * chans - 256)
            part = sw_ref[i, :, begin:begin + 256]
            if begin < chans * o:
                part = pltpu.roll(part, 256 - (chans * o - begin), 1)
            taps = jnp.where(head == o, part, taps)
        w_own[i, 0:3] = taps
    att[...] = jnp.zeros_like(att)
    conv_in[...] = jnp.zeros_like(conv_in)

    for f in range(FRAMES):
        loading(0, f).wait()
        loading(1, f).wait()
        for h in range(HEADS):
            local[h, f] = sums_frame(h, f, k_win, v_win)
    for h in range(HEADS):
        for f in range(1, FRAMES):
            local[h, f] = local[h, f] + local[h, f - 1]
        own[2 * h], own[2 * h + 1] = local[h, FRAMES - 1, :56], local[h, FRAMES - 1, 56:]
    pl.semaphore_wait(barrier, 15)
    scan = Scan(own, before, scratch[:6], False)
    scan.first()
    scan.second()
    scan.third()
    scan.last()

    def state(h, f):
        return rows_of(before, h) + local[h, f]

    for i, f in enumerate(ORDER):
        loading(2, f).wait()
        attend(f, q_win, state, att, inv)
        convolve(f, att, conv_in, w_own, act)
        for k in HOPS:
            strip(f, k).start()
        mine(f).start()
        pass_on((1, 2, 2, 2)[i])
    for i, f in enumerate(ORDER):
        loading(3, f).wait()
        query_grads(f, q_win, g_win, state, att, inv, gq_ref, ds)
        pass_on((1, 0, 1, 0)[i])
    for h in range(HEADS):
        for f in range(FRAMES - 2, -1, -1):
            ds[h, f] = ds[h, f] + ds[h, f + 1]
        own[2 * h], own[2 * h + 1] = ds[h, 0, :56], ds[h, 0, 56:]
    scan = Scan(own, after, scratch[6:], True)
    scan.first()
    pass_on(1)
    scan.second()
    pass_on(2)
    scan.third()
    pass_on(1)
    scan.last()
    pass_on(len(queue))

    def later(h, f):
        return rows_of(after, h) + ds[h, f]

    for f in range(FRAMES):
        key_grads(f, k_win, v_win, later, gk_ref, gv_ref)
    for f in range(FRAMES):
        mine(f).wait()
    for f in (0, 1):
        for k in HOPS:
            strip(f, k).wait_recv()
    for f in ORDER:
        for k in HOPS:
            strip(f, k).wait_send()
    for f in (2, 3):
        for k in (0,) + HOPS:
            forward(f, k).wait()


def main_call(q, k, v, g, weights):
    hbm = pl.BlockSpec(memory_space=pl.ANY)
    vmem = pl.BlockSpec(memory_space=pltpu.VMEM)
    wide = jax.ShapeDtypeStruct((HEADS * D, STRIDE * 3 + WIN), F32)
    window = pltpu.VMEM((FRAMES, HEADS * D, WIN), F32)
    states = pltpu.VMEM((HEADS, FRAMES, D, 128), F32)
    quarters = pltpu.VMEM((4, 56, 128), F32)
    return pl.pallas_call(
        main_kernel,
        out_shape=(
            wide,
            wide,
            wide,
            jax.ShapeDtypeStruct((STRIPS, FRAMES, CELLS, 256), F32),
            jax.ShapeDtypeStruct((STRIPS, 2, CELLS, 256), F32),
        ),
        in_specs=[hbm] * 4 + [vmem],
        out_specs=(vmem, vmem, vmem, hbm, hbm),
        scratch_shapes=[
            window, window, window, window,
            pltpu.VMEM((FRAMES, 256, WIN), F32),
            pltpu.VMEM((FRAMES, HEADS, 8, WIN), F32),
            pltpu.VMEM((BASE + WIN, 256), F32),
            pltpu.VMEM((FRAMES, STRIPS, CELLS, 256), F32),
            pltpu.VMEM((3, 8, 256), F32),
            states, states, quarters, quarters, quarters,
            pltpu.SemaphoreType.DMA((4, FRAMES)),
            pltpu.SemaphoreType.DMA((FRAMES, 8)),
            pltpu.SemaphoreType.DMA((FRAMES, 8)),
            pltpu.SemaphoreType.DMA((2, 8)),
            pltpu.SemaphoreType.DMA((2, 8)),
            pltpu.SemaphoreType.DMA((FRAMES,)),
        ] + SCAN_SCRATCH + SCAN_SCRATCH,
        compiler_params=pltpu.CompilerParams(collective_id=0, has_side_effects=True, vmem_limit_bytes=46 << 20),
        name="attention_exchange",
    )(q, k, v, g, weights)


def mix_group(base, count, halo_on, got, halo, tw_ref, tmp, mixed_ref):
    head = lax.axis_index("head")
    place = lax.broadcasted_iota(jnp.int32, (count, 128), 1)
    pending = [None] * FRAMES
    for owner in range(STRIPS):
        slot = head ^ owner
        for lane in range(2):
            lanes = slice(128 * lane, 128 * lane + 128)
            acts = [jnp.where(halo_on, halo[slot, i, pl.ds(base, count), lanes], 0.0) for i in range(2)]
            acts += [got[slot, f, pl.ds(base, count), lanes] for f in range(FRAMES)]
            w = [tw_ref[owner, i:i + 1, lanes] for i in range(3)]
            width = 128 if lane == 0 else 96
            tile, shift = divmod(224 * owner + 128 * lane, 128)
            for f in range(FRAMES):
                val = w[0] * acts[f + 2] + w[1] * acts[f + 1] + w[2] * acts[f]
                full = val
                if shift:
                    val = pltpu.roll(val, shift, 1)
                    full = jnp.where(place < shift, pending[f], val)
                if shift + width >= 128:
                    tmp[tile, pl.ds(f, count, stride=4), :] = full
                    pending[f] = val
                else:
                    pending[f] = full


def mix_kernel(got, halo, tw_ref, mixed_ref, tmp, tw):
    for owner in range(STRIPS):
        begin = min(224 * owner, 1792 - 256)
        part = tw_ref[:, begin:begin + 256]
        if begin < 224 * owner:
            part = pltpu.roll(part, 256 - (224 * owner - begin), 1)
        tw[owner, 0:3] = part
    halo_on = lax.axis_index("seg") > 0

    def group(base, count):
        mix_group(base, count, halo_on, got, halo, tw, tmp, mixed_ref)
        for i in range(count):
            for t in range(14):
                mixed_ref[base + i, :, 128 * t:128 * t + 128] = tmp[t, 4 * i:4 * i + 4, :]

    def step(i, carry):
        group(pl.multiple_of(8 * i, 8), 8)
        return carry

    lax.fori_loop(0, 12, step, 0)
    group(96, 4)


def mix(got, halo, tw):
    vmem = pl.BlockSpec(memory_space=pltpu.VMEM)
    return pl.pallas_call(
        mix_kernel,
        out_shape=jax.ShapeDtypeStruct((CELLS, FRAMES, 1792), F32),
        in_specs=[vmem] * 3,
        out_specs=vmem,
        scratch_shapes=[pltpu.VMEM((14, 32, 128), F32), pltpu.VMEM((STRIPS, 8, 256), F32)],
        compiler_params=pltpu.CompilerParams(vmem_limit_bytes=24 << 20),
        name="mix",
    )(got, halo, tw)


def body(query_feat, key_feat, value_feat, grad_out, spatial_weight, temporal_weight):
    gq, gk, gv, got, halo = main_call(query_feat, key_feat, value_feat, grad_out, spatial_weight)
    mixed = mix(got, halo, temporal_weight)
    mixed = jnp.transpose(mixed.reshape(ROWS, 5, FRAMES, STRIPS * HEADS * D), (2, 0, 1, 3))
    return gq, gk, gv, mixed


def solution(mesh):
    wide = P("head", "seg")
    in_specs = (wide, wide, wide, wide, P(), P())
    out_specs = (wide, wide, wide, P("seg", None, "head", None))
    return jax.shard_map(body, mesh=mesh, in_specs=in_specs, out_specs=out_specs, check_vma=False)
```

```python
import functools

import jax
import jax.numpy as jnp
from jax import lax
from jax.experimental import pallas as pl
from jax.experimental.pallas import tpu as pltpu
from jax.sharding import PartitionSpec as P

D = 112
ROWS = 20
COLS = 40
FRAMES = 4
STRIDE = 768
WIN = 896
HEADS = 2
STRIPS = 8
CELLS = 100
SPLIT = 80
PACKED = SPLIT + CELLS
CHUNKS = ((0, 256), (256, 256), (512, 256), (768, 128))
BASE = 136
MESH = pl.DeviceIdType.MESH
F32 = jnp.float32
BF16 = jnp.bfloat16
MAIN_LIMIT = 43 << 20
MIX_LIMIT = 43 << 20


def split(x):
    hi = x.astype(BF16)
    lo = (x - hi.astype(F32)).astype(BF16)
    return hi, lo


def nn(a, b):
    return lax.dot_general(a, b, (((1,), (0,)), ((), ())), preferred_element_type=F32)


def nt(a, b):
    return lax.dot_general(a, b, (((1,), (1,)), ((), ())), preferred_element_type=F32)


def pad_rows(x):
    return jnp.concatenate([x, jnp.zeros((16, x.shape[1]), x.dtype)], axis=0)


def left_mul(pair, b_hi, b_lo):
    return nn(pair, jnp.concatenate([b_hi, b_hi], axis=0)) + nn(pair[:, :128], b_lo)


def outer(a_hi, a_lo, b_hi, b_lo):
    both = nt(jnp.concatenate([a_hi, a_lo], axis=0), b_hi)
    rows = a_hi.shape[0]
    return both[:rows] + both[rows:] + nt(a_hi, b_lo)


def in_frame(frame, start, width):
    lane = lax.broadcasted_iota(jnp.int32, (1, width), 1) + start
    return (lane >= 32 * frame) & (lane < 32 * frame + ROWS * COLS)


def extra_row(row):
    place = lax.broadcasted_iota(jnp.int32, (16, row.shape[1]), 0)
    return jnp.where(place == 0, jnp.broadcast_to(row, (16, row.shape[1])), 0.0)


def side_by_side(x):
    hi, lo = split(x)
    return jnp.concatenate([hi, lo], axis=1)


def greet(devices):
    barrier = pltpu.get_barrier_semaphore()
    for dev in devices:
        pl.semaphore_signal(barrier, inc=1, device_id=dev, device_id_type=MESH)
    pl.semaphore_wait(barrier, len(devices))


SEGS = 16
PIECE = 16
SCAN_SCRATCH = [
    pltpu.VMEM((SEGS, PIECE, 128), F32),
    pltpu.VMEM((SEGS, PIECE, 128), F32),
    pltpu.SemaphoreType.DMA((2, SEGS)),
    pltpu.SemaphoreType.DMA((2, SEGS)),
]


def seg_peers():
    seg, head = lax.axis_index("seg"), lax.axis_index("head")
    return [((seg + k) % SEGS, head) for k in range(1, SEGS)]


class Scan:
    def __init__(self, own, result, scratch, reverse):
        self.own, self.result, self.reverse = own, result, reverse
        self.got, self.back, self.send, self.recv = scratch
        self.seg = lax.axis_index("seg")
        self.peers = seg_peers()

    def copy(self, phase, k, src, dst):
        return pltpu.make_async_remote_copy(
            src_ref=src, dst_ref=dst, send_sem=self.send.at[phase, k], recv_sem=self.recv.at[phase, k],
            device_id=self.peers[k - 1], device_id_type=MESH,
        )

    def first(self):
        self.c1 = [
            self.copy(0, k, self.own.at[(self.seg + k) % SEGS], self.got.at[self.seg]) for k in range(1, SEGS)
        ]
        for c in self.c1:
            c.start()
        self.got[self.seg] = self.own[self.seg]

    def second(self):
        for c in self.c1:
            c.wait()
        total = jnp.zeros((PIECE, 128), F32)
        order = range(SEGS - 1, -1, -1) if self.reverse else range(SEGS)
        for j in order:
            self.back[j] = total
            total = total + self.got[j]
        self.c2 = [
            self.copy(1, k, self.back.at[(self.seg + k) % SEGS], self.result.at[self.seg]) for k in range(1, SEGS)
        ]
        for c in self.c2:
            c.start()
        self.result[self.seg] = self.back[self.seg]

    def last(self):
        for c in self.c2:
            c.wait()


def ones_row(width):
    return extra_row(jnp.ones((1, width), F32)).astype(BF16)


def sums_frame(h, f, k_win, v_win):
    rows = slice(D * h, D * h + D)
    total = jnp.zeros((D, 128), F32)
    for start, width in CHUNKS:
        lanes = slice(start, start + width)
        ok = in_frame(f, start, width)
        k_hi, k_lo = split(jnp.where(ok, jnp.exp(k_win[f, rows, lanes]), 0.0))
        v_hi, v_lo = split(v_win[f, rows, lanes])
        v_hi = jnp.concatenate([v_hi, ones_row(width)], axis=0)
        total = total + outer(k_hi, k_lo, v_hi, pad_rows(v_lo))
    return total


def rows_of(ref, h):
    return jnp.concatenate([ref[7 * h + i] for i in range(7)], axis=0)


def put_rows(ref, h, value):
    for i in range(7):
        ref[7 * h + i] = value[PIECE * i:PIECE * i + PIECE]


def attend(f, q_win, state, att, inv):
    for h in range(HEADS):
        turned = side_by_side(pad_rows(state(h, f)).T)
        rows = slice(D * h, D * h + D)
        for start, width in CHUNKS:
            lanes = slice(start, start + width)
            q_hi, q_lo = split(jnp.exp(q_win[f, rows, lanes]))
            numer = left_mul(turned, pad_rows(q_hi), pad_rows(q_lo))
            inverse = 1.0 / numer[D:D + 1]
            att[f, rows, lanes] = jnp.where(in_frame(f, start, width), numer[:D] * inverse, 0.0)
            inv[f, h, 0:1, lanes] = inverse


def convolve(f, att, conv_in, w_own, send, rest):
    for m in range(WIN // 128):
        place = BASE - 32 * f + 128 * m
        conv_in[place:place + 128, :] = att[f, :, 128 * m:128 * m + 128].T
    edge = lax.broadcasted_iota(jnp.int32, (COLS, 128), 0)
    for lane in range(2):
        lanes = slice(128 * lane, 128 * lane + 128)
        taps = [[w_own[i, j:j + 1, lanes] for j in range(3)] for i in range(3)]
        for r in range(ROWS):
            lines = [conv_in[BASE + COLS * (r + i - 1):BASE + COLS * (r + i), lanes] for i in range(3)]
            cols = [taps[0][j] * lines[0] + taps[1][j] * lines[1] + taps[2][j] * lines[2] for j in range(3)]
            total = (
                cols[1]
                + jnp.where(edge == 0, 0.0, pltpu.roll(cols[0], 1, 0))
                + jnp.where(edge == COLS - 1, 0.0, pltpu.roll(cols[2], COLS - 1, 0))
            )
            half = 0.5 * total
            act = half + half * jnp.tanh(half)
            for j in range(STRIPS):
                part = act[5 * j:5 * j + 5]
                if lane == 0:
                    send[f, j, SPLIT + 5 * r:SPLIT + 5 * r + 5, :] = part
                elif 5 * r < SPLIT:
                    send[f, j, 5 * r:5 * r + 5, :] = part
                else:
                    rest[j, 5 * r - SPLIT:5 * r - SPLIT + 5, :] = part
    free = lax.broadcasted_iota(jnp.int32, (24, 128), 1) >= 96
    for j in range(STRIPS):
        for p in range(3):
            rows = slice(24 * p, 24 * p + 24)
            send[f, j, rows, :] = jnp.where(free, pltpu.roll(rest[j], 96 - 32 * p, 1), send[f, j, rows, :])


def place_of(f, start, width):
    return slice(STRIDE * f + start, STRIDE * f + start + width)


def query_grads(f, q_win, g_win, state, att, inv, gq_ref, ds):
    for h in range(HEADS):
        plain = side_by_side(state(h, f))
        rows = slice(D * h, D * h + D)
        grad_state = jnp.zeros((D, 128), F32)
        for start, width in CHUNKS:
            lanes = slice(start, start + width)
            ok = in_frame(f, start, width)
            feat = jnp.exp(q_win[f, rows, lanes])
            q_hi, q_lo = split(feat)
            inverse = inv[f, h, 0:1, lanes]
            grad = g_win[f, rows, lanes]
            slope = -jnp.sum(grad * att[f, rows, lanes], axis=0, keepdims=True) * inverse
            ext = jnp.where(ok, jnp.concatenate([grad * inverse, extra_row(slope)], axis=0), 0.0)
            n_hi, n_lo = split(ext)
            gq = left_mul(plain, n_hi, n_lo) * feat
            place = place_of(f, start, width)
            gq_ref[rows, place] = jnp.where(ok, gq, gq_ref[rows, place])
            grad_state = grad_state + outer(q_hi, q_lo, n_hi, n_lo)
        ds[h, f] = grad_state


def key_grads(f, k_win, v_win, state, gk_ref, gv_ref):
    for h in range(HEADS):
        plain = side_by_side(state(h, f))
        turned = side_by_side(pad_rows(state(h, f)).T)
        rows = slice(D * h, D * h + D)
        for start, width in CHUNKS:
            lanes = slice(start, start + width)
            ok = in_frame(f, start, width)
            feat = jnp.exp(k_win[f, rows, lanes])
            k_hi, k_lo = split(feat)
            v_hi, v_lo = split(v_win[f, rows, lanes])
            v_hi = jnp.concatenate([v_hi, ones_row(width)], axis=0)
            gk = left_mul(plain, v_hi, pad_rows(v_lo)) * feat
            gv = left_mul(turned, pad_rows(k_hi), pad_rows(k_lo))[:D]
            place = place_of(f, start, width)
            gk_ref[rows, place] = jnp.where(ok, gk, gk_ref[rows, place])
            gv_ref[rows, place] = jnp.where(ok, gv, gv_ref[rows, place])


ORDER = (2, 3, 0, 1)
HOPS = (1, 2, 6, 3, 5, 7, 4)


def main_kernel(q_ref, k_ref, v_ref, g_ref, sw_ref, gq_ref, gk_ref, gv_ref, got_ref, halo_ref,
                q_win, k_win, v_win, g_win, att, inv, conv_in, act, rest, w_own, local, ds, own, before, after,
                load, send, recv, fsend, frecv, lsem, *scratch):
    seg, head = lax.axis_index("seg"), lax.axis_index("head")
    peers = [(seg, head ^ k) for k in range(1, 8)]
    up = ((seg + 1) % SEGS, head)
    barrier = pltpu.get_barrier_semaphore()
    for dev in seg_peers() + peers:
        pl.semaphore_signal(barrier, inc=1, device_id=dev, device_id_type=MESH)

    wins = ((k_ref, k_win), (v_ref, v_win), (q_ref, q_win), (g_ref, g_win))

    def loading(i, f):
        src, dst = wins[i]
        return pltpu.make_async_copy(src.at[:, STRIDE * f:STRIDE * f + WIN], dst.at[f], load.at[i, f])

    for f in range(FRAMES):
        for i in range(2):
            loading(i, f).start()
    for i in (2, 3):
        for f in ORDER:
            loading(i, f).start()

    def strip(f, k):
        return pltpu.make_async_remote_copy(
            src_ref=act.at[f, head ^ k], dst_ref=got_ref.at[k, f], send_sem=send.at[f, k], recv_sem=recv.at[f, k],
            device_id=(seg, head ^ k), device_id_type=MESH,
        )

    def forward(f, k):
        src = act.at[f, head] if k == 0 else got_ref.at[k, f]
        return pltpu.make_async_remote_copy(
            src_ref=src, dst_ref=halo_ref.at[k, f - 2], send_sem=fsend.at[f - 2, k], recv_sem=frecv.at[f - 2, k],
            device_id=up, device_id_type=MESH,
        )

    def mine(f):
        return pltpu.make_async_copy(act.at[f, head], got_ref.at[0, f], lsem.at[f])

    queue = [(2, 0), (3, 0), (2, 1), (3, 1)] + [(2, k) for k in HOPS[1:]] + [(3, k) for k in HOPS[1:]]

    def pass_on(count):
        for f, k in queue[:count]:
            if k:
                strip(f, k).wait_recv()
            forward(f, k).start()
        del queue[:count]

    lanes = pl.ds(0, 256)
    chans = HEADS * D
    for i in range(3):
        taps = sw_ref[i, :, :256]
        for o in range(1, STRIPS):
            begin = min(chans * o, STRIPS * chans - 256)
            part = sw_ref[i, :, begin:begin + 256]
            if begin < chans * o:
                part = pltpu.roll(part, 256 - (chans * o - begin), 1)
            taps = jnp.where(head == o, part, taps)
        w_own[i, 0:3] = taps
    for f in range(FRAMES):
        att[f, HEADS * D:, :] = jnp.zeros((32, WIN), F32)
    conv_in[BASE + 800:, :] = jnp.zeros((WIN - 800, 256), F32)
    for p in (SEGS - 2, SEGS - 1):
        own[p] = jnp.zeros((PIECE, 128), F32)

    for f in range(FRAMES):
        loading(0, f).wait()
        loading(1, f).wait()
        for h in range(HEADS):
            local[h, f] = sums_frame(h, f, k_win, v_win)
    for h in range(HEADS):
        for f in range(1, FRAMES):
            local[h, f] = local[h, f] + local[h, f - 1]
        put_rows(own, h, local[h, FRAMES - 1])
    pl.semaphore_wait(barrier, SEGS - 1 + 7)
    scan = Scan(own, before, scratch[:4], False)
    scan.first()
    scan.second()
    scan.last()

    def state(h, f):
        return rows_of(before, h) + local[h, f]

    for i, f in enumerate(ORDER):
        loading(2, f).wait()
        attend(f, q_win, state, att, inv)
        convolve(f, att, conv_in, w_own, act, rest)
        for k in HOPS:
            strip(f, k).start()
        mine(f).start()
        pass_on((1, 2, 2, 2)[i])
    for i, f in enumerate(ORDER):
        loading(3, f).wait()
        query_grads(f, q_win, g_win, state, att, inv, gq_ref, ds)
        pass_on((1, 0, 1, 0)[i])
    for h in range(HEADS):
        for f in range(FRAMES - 2, -1, -1):
            ds[h, f] = ds[h, f] + ds[h, f + 1]
        put_rows(own, h, ds[h, 0])
    scan = Scan(own, after, scratch[4:], True)
    scan.first()
    pass_on(2)
    scan.second()
    pass_on(2)
    scan.last()
    pass_on(len(queue))

    def later(h, f):
        return rows_of(after, h) + ds[h, f]

    for f in range(FRAMES):
        key_grads(f, k_win, v_win, later, gk_ref, gv_ref)
    for f in range(FRAMES):
        mine(f).wait()
    for f in (0, 1):
        for k in HOPS:
            strip(f, k).wait_recv()
    for f in ORDER:
        for k in HOPS:
            strip(f, k).wait_send()
    for f in (2, 3):
        for k in (0,) + HOPS:
            forward(f, k).wait()


def main_call(q, k, v, g, weights):
    hbm = pl.BlockSpec(memory_space=pl.ANY)
    vmem = pl.BlockSpec(memory_space=pltpu.VMEM)
    wide = jax.ShapeDtypeStruct((HEADS * D, STRIDE * 3 + WIN), F32)
    window = pltpu.VMEM((FRAMES, HEADS * D, WIN), F32)
    states = pltpu.VMEM((HEADS, FRAMES, D, 128), F32)
    pieces = pltpu.VMEM((SEGS, PIECE, 128), F32)
    return pl.pallas_call(
        main_kernel,
        out_shape=(
            wide,
            wide,
            wide,
            jax.ShapeDtypeStruct((STRIPS, FRAMES, PACKED, 128), F32),
            jax.ShapeDtypeStruct((STRIPS, 2, PACKED, 128), F32),
        ),
        in_specs=[hbm] * 4 + [vmem],
        out_specs=(vmem, vmem, vmem, hbm, hbm),
        scratch_shapes=[
            window, window, window, window,
            pltpu.VMEM((FRAMES, 256, WIN), F32),
            pltpu.VMEM((FRAMES, HEADS, 8, WIN), F32),
            pltpu.VMEM((BASE + WIN, 256), F32),
            pltpu.VMEM((FRAMES, STRIPS, PACKED, 128), F32),
            pltpu.VMEM((STRIPS, 24, 128), F32),
            pltpu.VMEM((3, 8, 256), F32),
            states, states, pieces, pieces, pieces,
            pltpu.SemaphoreType.DMA((4, FRAMES)),
            pltpu.SemaphoreType.DMA((FRAMES, 8)),
            pltpu.SemaphoreType.DMA((FRAMES, 8)),
            pltpu.SemaphoreType.DMA((2, 8)),
            pltpu.SemaphoreType.DMA((2, 8)),
            pltpu.SemaphoreType.DMA((FRAMES,)),
        ] + SCAN_SCRATCH + SCAN_SCRATCH,
        compiler_params=pltpu.CompilerParams(collective_id=0, has_side_effects=True, vmem_limit_bytes=MAIN_LIMIT),
        name="attention_exchange",
    )(q, k, v, g, weights)


def cells(ref, index, base, count, lane):
    if lane == 0:
        return ref[index + (pl.ds(SPLIT + base, count),)]
    if not isinstance(base, int):
        return ref[index + (pl.ds(base, count),)]
    place = lax.broadcasted_iota(jnp.int32, (count, 128), 1)
    parts = [
        pltpu.roll(ref[index + (slice(24 * p + base - SPLIT, 24 * p + base - SPLIT + count),)], 32 + 32 * p, 1)
        for p in range(3)
    ]
    return jnp.where(place < 32, parts[0], jnp.where(place < 64, parts[1], parts[2]))


def mix_group(base, count, halo_on, got, halo, tw_ref, tmp):
    head = lax.axis_index("head")
    place = lax.broadcasted_iota(jnp.int32, (count, 128), 1)
    pending = [None] * FRAMES
    for owner in range(STRIPS):
        slot = head ^ owner
        for lane in range(2):
            acts = [jnp.where(halo_on, cells(halo, (slot, i), base, count, lane), 0.0) for i in range(2)]
            acts += [cells(got, (slot, f), base, count, lane) for f in range(FRAMES)]
            w = [tw_ref[owner, i:i + 1, 128 * lane:128 * lane + 128] for i in range(3)]
            width = 128 if lane == 0 else 96
            tile, shift = divmod(224 * owner + 128 * lane, 128)
            for f in range(FRAMES):
                val = w[0] * acts[f + 2] + w[1] * acts[f + 1] + w[2] * acts[f]
                full = val
                if shift:
                    val = pltpu.roll(val, shift, 1)
                    full = jnp.where(place < shift, pending[f], val)
                if shift + width >= 128:
                    tmp[tile, pl.ds(f, count, stride=4), :] = full
                    pending[f] = val
                else:
                    pending[f] = full


def mix_kernel(got_ref, halo, tw_ref, gq, gk, gv, gq_out, gk_out, gv_out, mixed_out, got, tmp, tw, mixed, gsem, sem, msem):
    parts = [
        pltpu.make_async_copy(got_ref.at[:, :, rows], got.at[:, :, rows], gsem.at[i])
        for i, rows in enumerate((slice(0, SPLIT), slice(SPLIT, 120), slice(120, PACKED)))
    ]
    for c in parts:
        c.start()
    plain = [
        pltpu.make_async_copy(src, dst, sem.at[i])
        for i, (src, dst) in enumerate(((gq, gq_out), (gk, gk_out), (gv, gv_out)))
    ]
    for c in plain:
        c.start()
    for owner in range(STRIPS):
        begin = min(224 * owner, 1792 - 256)
        part = tw_ref[:, begin:begin + 256]
        if begin < 224 * owner:
            part = pltpu.roll(part, 256 - (224 * owner - begin), 1)
        tw[owner, 0:3] = part
    halo_on = lax.axis_index("seg") > 0

    def leaving(base, count, i):
        rows = pl.ds(base, count)
        return pltpu.make_async_copy(mixed.at[rows], mixed_out.at[rows], msem.at[i])

    def group(base, count, g):
        mix_group(base, count, halo_on, got, halo, tw, tmp)
        for i in range(count):
            for t in range(14):
                mixed[base + i, :, 128 * t:128 * t + 128] = tmp[t, 4 * i:4 * i + 4, :]
        leaving(base, count, g).start()

    def step(i, carry):
        group(pl.multiple_of(8 * i, 8), 8, i)
        return carry

    parts[0].wait()
    parts[1].wait()
    lax.fori_loop(0, 5, step, 0)
    parts[2].wait()
    lax.fori_loop(5, 10, step, 0)
    group(80, 8, 10)
    group(88, 8, 11)
    group(96, 4, 12)
    for g in range(13):
        leaving(8 * g, 4 if g == 12 else 8, g).wait()
    for c in plain:
        c.wait()


def mix(got, halo, tw, gq, gk, gv):
    vmem = pl.BlockSpec(memory_space=pltpu.VMEM)
    hbm = pl.BlockSpec(memory_space=pl.ANY)
    wide = jax.ShapeDtypeStruct(gq.shape, F32)
    return pl.pallas_call(
        mix_kernel,
        out_shape=(wide, wide, wide, jax.ShapeDtypeStruct((CELLS, FRAMES, 1792), F32)),
        in_specs=[hbm] + [vmem] * 5,
        out_specs=(hbm, hbm, hbm, hbm),
        scratch_shapes=[
            pltpu.VMEM((STRIPS, FRAMES, PACKED, 128), F32),
            pltpu.VMEM((14, 32, 128), F32),
            pltpu.VMEM((STRIPS, 8, 256), F32),
            pltpu.VMEM((CELLS, FRAMES, 1792), F32),
            pltpu.SemaphoreType.DMA((3,)),
            pltpu.SemaphoreType.DMA((3,)),
            pltpu.SemaphoreType.DMA((13,)),
        ],
        compiler_params=pltpu.CompilerParams(vmem_limit_bytes=MIX_LIMIT),
        name="mix",
    )(got, halo, tw, gq, gk, gv)


def body(query_feat, key_feat, value_feat, grad_out, spatial_weight, temporal_weight):
    gq, gk, gv, got, halo = main_call(query_feat, key_feat, value_feat, grad_out, spatial_weight)
    gq, gk, gv, mixed = mix(got, halo, temporal_weight, gq, gk, gv)
    mixed = jnp.transpose(mixed.reshape(ROWS, 5, FRAMES, STRIPS * HEADS * D), (2, 0, 1, 3))
    return gq, gk, gv, mixed


def solution(mesh):
    wide = P("head", "seg")
    in_specs = (wide, wide, wide, wide, P(), P())
    out_specs = (wide, wide, wide, P("seg", None, "head", None))
    return jax.shard_map(body, mesh=mesh, in_specs=in_specs, out_specs=out_specs, check_vma=False)
```

```python
import functools

import jax
import jax.numpy as jnp
from jax import lax
from jax.experimental import pallas as pl
from jax.experimental.pallas import tpu as pltpu
from jax.sharding import PartitionSpec as P

D = 112
ROWS = 20
COLS = 40
FRAMES = 4
STRIDE = 768
WIN = 896
HEADS = 2
STRIPS = 8
CELLS = 100
SPLIT = 80
PACKED = SPLIT + CELLS
CHUNKS = ((0, 256), (256, 256), (512, 256), (768, 128))
BASE = 136
MESH = pl.DeviceIdType.MESH
F32 = jnp.float32
BF16 = jnp.bfloat16
MAIN_LIMIT = 39 << 20
MIX_LIMIT = 39 << 20


def split(x):
    hi = x.astype(BF16)
    lo = (x - hi.astype(F32)).astype(BF16)
    return hi, lo


def nn(a, b):
    return lax.dot_general(a, b, (((1,), (0,)), ((), ())), preferred_element_type=F32)


def nt(a, b):
    return lax.dot_general(a, b, (((1,), (1,)), ((), ())), preferred_element_type=F32)


def pad_rows(x):
    return jnp.concatenate([x, jnp.zeros((16, x.shape[1]), x.dtype)], axis=0)


def left_mul(pair, b_hi, b_lo):
    return nn(pair, jnp.concatenate([b_hi, b_hi], axis=0)) + nn(pair[:, :128], b_lo)


def outer(a_hi, a_lo, b_hi, b_lo):
    both = nt(jnp.concatenate([a_hi, a_lo], axis=0), b_hi)
    rows = a_hi.shape[0]
    return both[:rows] + both[rows:] + nt(a_hi, b_lo)


def in_frame(frame, start, width):
    lane = lax.broadcasted_iota(jnp.int32, (1, width), 1) + start
    return (lane >= 32 * frame) & (lane < 32 * frame + ROWS * COLS)


def extra_row(row):
    place = lax.broadcasted_iota(jnp.int32, (16, row.shape[1]), 0)
    return jnp.where(place == 0, jnp.broadcast_to(row, (16, row.shape[1])), 0.0)


def side_by_side(x):
    hi, lo = split(x)
    return jnp.concatenate([hi, lo], axis=1)


def greet(devices):
    barrier = pltpu.get_barrier_semaphore()
    for dev in devices:
        pl.semaphore_signal(barrier, inc=1, device_id=dev, device_id_type=MESH)
    pl.semaphore_wait(barrier, len(devices))


SEGS = 16
PIECE = 16
SCAN_SCRATCH = [
    pltpu.VMEM((SEGS, PIECE, 128), F32),
    pltpu.VMEM((SEGS, PIECE, 128), F32),
    pltpu.SemaphoreType.DMA((2, SEGS)),
    pltpu.SemaphoreType.DMA((2, SEGS)),
]


def seg_peers():
    seg, head = lax.axis_index("seg"), lax.axis_index("head")
    return [((seg + k) % SEGS, head) for k in range(1, SEGS)]


class Scan:
    def __init__(self, own, result, scratch, reverse):
        self.own, self.result, self.reverse = own, result, reverse
        self.got, self.back, self.send, self.recv = scratch
        self.seg = lax.axis_index("seg")
        self.peers = seg_peers()

    def copy(self, phase, k, src, dst):
        return pltpu.make_async_remote_copy(
            src_ref=src, dst_ref=dst, send_sem=self.send.at[phase, k], recv_sem=self.recv.at[phase, k],
            device_id=self.peers[k - 1], device_id_type=MESH,
        )

    def first(self):
        self.c1 = [
            self.copy(0, k, self.own.at[(self.seg + k) % SEGS], self.got.at[self.seg]) for k in range(1, SEGS)
        ]
        for c in self.c1:
            c.start()
        self.got[self.seg] = self.own[self.seg]

    def second(self):
        for c in self.c1:
            c.wait_recv()
        total = jnp.zeros((PIECE, 128), F32)
        order = range(SEGS - 1, -1, -1) if self.reverse else range(SEGS)
        for j in order:
            self.back[j] = total
            total = total + self.got[j]
        self.c2 = [
            self.copy(1, k, self.back.at[(self.seg + k) % SEGS], self.result.at[self.seg]) for k in range(1, SEGS)
        ]
        for c in self.c2:
            c.start()
        self.result[self.seg] = self.back[self.seg]

    def last(self):
        for c in self.c2:
            c.wait_recv()

    def drain(self):
        for c in self.c1 + self.c2:
            c.wait_send()


def ones_row(width):
    return extra_row(jnp.ones((1, width), F32)).astype(BF16)


def sums_frame(h, f, k_win, v_win):
    rows = slice(D * h, D * h + D)
    total = jnp.zeros((D, 128), F32)
    for start, width in CHUNKS:
        lanes = slice(start, start + width)
        ok = in_frame(f, start, width)
        k_hi, k_lo = split(jnp.where(ok, jnp.exp(k_win[f, rows, lanes]), 0.0))
        v_hi, v_lo = split(v_win[f, rows, lanes])
        v_hi = jnp.concatenate([v_hi, ones_row(width)], axis=0)
        total = total + outer(k_hi, k_lo, v_hi, pad_rows(v_lo))
    return total


def rows_of(ref, h):
    return jnp.concatenate([ref[7 * h + i] for i in range(7)], axis=0)


def put_rows(ref, h, value):
    for i in range(7):
        ref[7 * h + i] = value[PIECE * i:PIECE * i + PIECE]


def attend(f, q_win, state, att, inv):
    for h in range(HEADS):
        turned = side_by_side(pad_rows(state(h, f)).T)
        rows = slice(D * h, D * h + D)
        for start, width in CHUNKS:
            lanes = slice(start, start + width)
            q_hi, q_lo = split(jnp.exp(q_win[f, rows, lanes]))
            numer = left_mul(turned, pad_rows(q_hi), pad_rows(q_lo))
            inverse = 1.0 / numer[D:D + 1]
            att[f, rows, lanes] = jnp.where(in_frame(f, start, width), numer[:D] * inverse, 0.0)
            inv[f, h, 0:1, lanes] = inverse


def convolve(f, att, conv_in, w_own, send, rest):
    for m in range(WIN // 128):
        place = BASE - 32 * f + 128 * m
        conv_in[place:place + 128, :] = att[f, :, 128 * m:128 * m + 128].T
    edge = lax.broadcasted_iota(jnp.int32, (COLS, 128), 0)
    for lane in range(2):
        lanes = slice(128 * lane, 128 * lane + 128)
        taps = [[w_own[i, j:j + 1, lanes] for j in range(3)] for i in range(3)]
        for r in range(ROWS):
            lines = [conv_in[BASE + COLS * (r + i - 1):BASE + COLS * (r + i), lanes] for i in range(3)]
            cols = [taps[0][j] * lines[0] + taps[1][j] * lines[1] + taps[2][j] * lines[2] for j in range(3)]
            total = (
                cols[1]
                + jnp.where(edge == 0, 0.0, pltpu.roll(cols[0], 1, 0))
                + jnp.where(edge == COLS - 1, 0.0, pltpu.roll(cols[2], COLS - 1, 0))
            )
            half = 0.5 * total
            act = half + half * jnp.tanh(half)
            for j in range(STRIPS):
                part = act[5 * j:5 * j + 5]
                if lane == 0:
                    send[f, j, SPLIT + 5 * r:SPLIT + 5 * r + 5, :] = part
                elif 5 * r < SPLIT:
                    send[f, j, 5 * r:5 * r + 5, :] = part
                else:
                    rest[j, 5 * r - SPLIT:5 * r - SPLIT + 5, :] = part
    free = lax.broadcasted_iota(jnp.int32, (24, 128), 1) >= 96
    for j in range(STRIPS):
        for p in range(3):
            rows = slice(24 * p, 24 * p + 24)
            send[f, j, rows, :] = jnp.where(free, pltpu.roll(rest[j], 96 - 32 * p, 1), send[f, j, rows, :])


def place_of(f, start, width):
    return slice(STRIDE * f + start, STRIDE * f + start + width)


def query_grads(f, q_win, g_win, state, att, inv, gq_ref, ds):
    for h in range(HEADS):
        plain = side_by_side(state(h, f))
        rows = slice(D * h, D * h + D)
        grad_state = jnp.zeros((D, 128), F32)
        for start, width in CHUNKS:
            lanes = slice(start, start + width)
            ok = in_frame(f, start, width)
            feat = jnp.exp(q_win[f, rows, lanes])
            q_hi, q_lo = split(feat)
            inverse = inv[f, h, 0:1, lanes]
            grad = g_win[f, rows, lanes]
            slope = -jnp.sum(grad * att[f, rows, lanes], axis=0, keepdims=True) * inverse
            ext = jnp.where(ok, jnp.concatenate([grad * inverse, extra_row(slope)], axis=0), 0.0)
            n_hi, n_lo = split(ext)
            gq = left_mul(plain, n_hi, n_lo) * feat
            place = place_of(f, start, width)
            gq_ref[rows, place] = jnp.where(ok, gq, gq_ref[rows, place])
            grad_state = grad_state + outer(q_hi, q_lo, n_hi, n_lo)
        ds[h, f] = grad_state


def key_grads(f, k_win, v_win, state, gk_ref, gv_ref):
    for h in range(HEADS):
        plain = side_by_side(state(h, f))
        turned = side_by_side(pad_rows(state(h, f)).T)
        rows = slice(D * h, D * h + D)
        for start, width in CHUNKS:
            lanes = slice(start, start + width)
            ok = in_frame(f, start, width)
            feat = jnp.exp(k_win[f, rows, lanes])
            k_hi, k_lo = split(feat)
            v_hi, v_lo = split(v_win[f, rows, lanes])
            v_hi = jnp.concatenate([v_hi, ones_row(width)], axis=0)
            gk = left_mul(plain, v_hi, pad_rows(v_lo)) * feat
            gv = left_mul(turned, pad_rows(k_hi), pad_rows(k_lo))[:D]
            place = place_of(f, start, width)
            gk_ref[rows, place] = jnp.where(ok, gk, gk_ref[rows, place])
            gv_ref[rows, place] = jnp.where(ok, gv, gv_ref[rows, place])


ORDER = (2, 3, 0, 1)
HOPS = (1, 2, 6, 3, 5, 7, 4)


def main_kernel(q_ref, k_ref, v_ref, g_ref, sw_ref, gq_ref, gk_ref, gv_ref, got_early, got_late, halo_ref,
                q_win, k_win, v_win, g_win, att, inv, conv_in, act, rest, w_own, local, ds, own, before, after,
                load, send, recv, fsend, frecv, lsem, *scratch):
    seg, head = lax.axis_index("seg"), lax.axis_index("head")
    peers = [(seg, head ^ k) for k in range(1, 8)]
    up = ((seg + 1) % SEGS, head)
    barrier = pltpu.get_barrier_semaphore()
    for dev in seg_peers() + peers:
        pl.semaphore_signal(barrier, inc=1, device_id=dev, device_id_type=MESH)

    wins = ((k_ref, k_win), (v_ref, v_win), (q_ref, q_win), (g_ref, g_win))

    def loading(i, f):
        src, dst = wins[i]
        return pltpu.make_async_copy(src.at[:, STRIDE * f:STRIDE * f + WIN], dst.at[f], load.at[i, f])

    for f in range(FRAMES):
        for i in range(2):
            loading(i, f).start()

    def got_at(k, f):
        return (got_early if f >= 2 else got_late).at[k, f % 2]

    def strip(f, k):
        return pltpu.make_async_remote_copy(
            src_ref=act.at[f, head ^ k], dst_ref=got_at(k, f), send_sem=send.at[f, k], recv_sem=recv.at[f, k],
            device_id=(seg, head ^ k), device_id_type=MESH,
        )

    def forward(f, k):
        src = act.at[f, head] if k == 0 else got_at(k, f)
        return pltpu.make_async_remote_copy(
            src_ref=src, dst_ref=halo_ref.at[k, f - 2], send_sem=fsend.at[f - 2, k], recv_sem=frecv.at[f - 2, k],
            device_id=up, device_id_type=MESH,
        )

    def mine(f):
        return pltpu.make_async_copy(act.at[f, head], got_at(0, f), lsem.at[f])

    queue = [(2, 0), (3, 0), (2, 1), (3, 1)] + [(2, k) for k in HOPS[1:]] + [(3, k) for k in HOPS[1:]]

    def pass_on(count):
        for f, k in queue[:count]:
            if k:
                strip(f, k).wait_recv()
            forward(f, k).start()
        del queue[:count]

    for p in (SEGS - 2, SEGS - 1):
        own[p] = jnp.zeros((PIECE, 128), F32)

    for f in range(FRAMES):
        loading(0, f).wait()
        loading(1, f).wait()
        for h in range(HEADS):
            local[h, f] = sums_frame(h, f, k_win, v_win)
    for h in range(HEADS):
        for f in range(1, FRAMES):
            local[h, f] = local[h, f] + local[h, f - 1]
        put_rows(own, h, local[h, FRAMES - 1])
    pl.semaphore_wait(barrier, SEGS - 1 + 7)
    scan = Scan(own, before, scratch[:4], False)
    scan.first()
    for i in (2, 3):
        for f in ORDER:
            loading(i, f).start()
    lanes = pl.ds(0, 256)
    chans = HEADS * D
    for i in range(3):
        taps = sw_ref[i, :, :256]
        for o in range(1, STRIPS):
            begin = min(chans * o, STRIPS * chans - 256)
            part = sw_ref[i, :, begin:begin + 256]
            if begin < chans * o:
                part = pltpu.roll(part, 256 - (chans * o - begin), 1)
            taps = jnp.where(head == o, part, taps)
        w_own[i, 0:3] = taps
    for f in range(FRAMES):
        att[f, HEADS * D:, :] = jnp.zeros((32, WIN), F32)
    conv_in[BASE + 800:, :] = jnp.zeros((WIN - 800, 256), F32)
    scan.second()
    scan.last()

    def state(h, f):
        return rows_of(before, h) + local[h, f]

    for i, f in enumerate(ORDER):
        loading(2, f).wait()
        attend(f, q_win, state, att, inv)
        convolve(f, att, conv_in, w_own, act, rest)
        for k in HOPS:
            strip(f, k).start()
        mine(f).start()
        pass_on((1, 2, 2, 2)[i])
    for i, f in enumerate(ORDER):
        loading(3, f).wait()
        query_grads(f, q_win, g_win, state, att, inv, gq_ref, ds)
    scan.drain()
    for h in range(HEADS):
        for f in range(FRAMES - 2, -1, -1):
            ds[h, f] = ds[h, f] + ds[h, f + 1]
        put_rows(own, h, ds[h, 0])
    scan = Scan(own, after, scratch[4:], True)
    scan.first()
    pass_on(2)
    scan.second()
    pass_on(2)
    scan.last()
    pass_on(4)

    def later(h, f):
        return rows_of(after, h) + ds[h, f]

    for f in range(FRAMES):
        key_grads(f, k_win, v_win, later, gk_ref, gv_ref)
        pass_on(1)
    pass_on(len(queue))
    scan.drain()
    for f in range(FRAMES):
        mine(f).wait()
    for f in (0, 1):
        for k in HOPS:
            strip(f, k).wait_recv()
    for f in ORDER:
        for k in HOPS:
            strip(f, k).wait_send()
    for f in (2, 3):
        for k in (0,) + HOPS:
            forward(f, k).wait()


def main_call(q, k, v, g, weights):
    hbm = pl.BlockSpec(memory_space=pl.ANY)
    vmem = pl.BlockSpec(memory_space=pltpu.VMEM)
    wide = jax.ShapeDtypeStruct((HEADS * D, STRIDE * 3 + WIN), F32)
    half = jax.ShapeDtypeStruct((STRIPS, 2, PACKED, 128), F32)
    window = pltpu.VMEM((FRAMES, HEADS * D, WIN), F32)
    states = pltpu.VMEM((HEADS, FRAMES, D, 128), F32)
    pieces = pltpu.VMEM((SEGS, PIECE, 128), F32)
    return pl.pallas_call(
        main_kernel,
        out_shape=(
            wide,
            wide,
            wide,
            half,
            half,
            half,
        ),
        in_specs=[hbm] * 4 + [vmem],
        out_specs=(vmem, vmem, vmem, hbm, hbm, hbm),
        scratch_shapes=[
            window, window, window, window,
            pltpu.VMEM((FRAMES, 256, WIN), F32),
            pltpu.VMEM((FRAMES, HEADS, 8, WIN), F32),
            pltpu.VMEM((BASE + WIN, 256), F32),
            pltpu.VMEM((FRAMES, STRIPS, PACKED, 128), F32),
            pltpu.VMEM((STRIPS, 24, 128), F32),
            pltpu.VMEM((3, 8, 256), F32),
            states, states, pieces, pieces, pieces,
            pltpu.SemaphoreType.DMA((4, FRAMES)),
            pltpu.SemaphoreType.DMA((FRAMES, 8)),
            pltpu.SemaphoreType.DMA((FRAMES, 8)),
            pltpu.SemaphoreType.DMA((2, 8)),
            pltpu.SemaphoreType.DMA((2, 8)),
            pltpu.SemaphoreType.DMA((FRAMES,)),
        ] + SCAN_SCRATCH + SCAN_SCRATCH,
        compiler_params=pltpu.CompilerParams(collective_id=0, has_side_effects=True, vmem_limit_bytes=MAIN_LIMIT),
        name="attention_exchange",
    )(q, k, v, g, weights)


def cells(ref, index, base, count, lane):
    if lane == 0:
        return ref[index + (pl.ds(SPLIT + base, count),)]
    if not isinstance(base, int):
        return ref[index + (pl.ds(base, count),)]
    place = lax.broadcasted_iota(jnp.int32, (count, 128), 1)
    parts = [
        pltpu.roll(ref[index + (slice(24 * p + base - SPLIT, 24 * p + base - SPLIT + count),)], 32 + 32 * p, 1)
        for p in range(3)
    ]
    return jnp.where(place < 32, parts[0], jnp.where(place < 64, parts[1], parts[2]))


def mix_group(base, count, halo_on, got, halo, tw_ref, tmp):
    head = lax.axis_index("head")
    place = lax.broadcasted_iota(jnp.int32, (count, 128), 1)
    pending = [None] * FRAMES
    for owner in range(STRIPS):
        slot = head ^ owner
        for lane in range(2):
            acts = [jnp.where(halo_on, cells(halo, (slot, i), base, count, lane), 0.0) for i in range(2)]
            acts += [cells(got[f // 2], (slot, f % 2), base, count, lane) for f in range(FRAMES)]
            w = [tw_ref[owner, i:i + 1, 128 * lane:128 * lane + 128] for i in range(3)]
            width = 128 if lane == 0 else 96
            tile, shift = divmod(224 * owner + 128 * lane, 128)
            for f in range(FRAMES):
                val = w[0] * acts[f + 2] + w[1] * acts[f + 1] + w[2] * acts[f]
                full = val
                if shift:
                    val = pltpu.roll(val, shift, 1)
                    full = jnp.where(place < shift, pending[f], val)
                if shift + width >= 128:
                    tmp[tile, pl.ds(f, count, stride=4), :] = full
                    pending[f] = val
                else:
                    pending[f] = full


def mix_kernel(got_early, got_late, halo, tw_ref, gq, gk, gv, gq_out, gk_out, gv_out, mixed_out, tmp, tw, mixed, sem, msem):
    plain = [
        pltpu.make_async_copy(src, dst, sem.at[i])
        for i, (src, dst) in enumerate(((gq, gq_out), (gk, gk_out), (gv, gv_out)))
    ]
    for c in plain:
        c.start()
    for owner in range(STRIPS):
        begin = min(224 * owner, 1792 - 256)
        part = tw_ref[:, begin:begin + 256]
        if begin < 224 * owner:
            part = pltpu.roll(part, 256 - (224 * owner - begin), 1)
        tw[owner, 0:3] = part
    halo_on = lax.axis_index("seg") > 0

    def leaving(base, count, i):
        rows = pl.ds(base, count)
        return pltpu.make_async_copy(mixed.at[rows], mixed_out.at[rows], msem.at[i])

    def group(base, count, g):
        mix_group(base, count, halo_on, (got_late, got_early), halo, tw, tmp)
        for i in range(count):
            for t in range(14):
                mixed[base + i, :, 128 * t:128 * t + 128] = tmp[t, 4 * i:4 * i + 4, :]
        leaving(base, count, g).start()

    def step(i, carry):
        group(pl.multiple_of(8 * i, 8), 8, i)
        return carry

    lax.fori_loop(0, 10, step, 0)
    group(80, 8, 10)
    group(88, 8, 11)
    group(96, 4, 12)
    for g in range(13):
        leaving(8 * g, 4 if g == 12 else 8, g).wait()
    for c in plain:
        c.wait()


def mix(early, late, halo, tw, gq, gk, gv):
    vmem = pl.BlockSpec(memory_space=pltpu.VMEM)
    hbm = pl.BlockSpec(memory_space=pl.ANY)
    wide = jax.ShapeDtypeStruct(gq.shape, F32)
    return pl.pallas_call(
        mix_kernel,
        out_shape=(wide, wide, wide, jax.ShapeDtypeStruct((CELLS, FRAMES, 1792), F32)),
        in_specs=[vmem] * 7,
        out_specs=(hbm, hbm, hbm, hbm),
        scratch_shapes=[
            pltpu.VMEM((14, 32, 128), F32),
            pltpu.VMEM((STRIPS, 8, 256), F32),
            pltpu.VMEM((CELLS, FRAMES, 1792), F32),
            pltpu.SemaphoreType.DMA((3,)),
            pltpu.SemaphoreType.DMA((13,)),
        ],
        compiler_params=pltpu.CompilerParams(vmem_limit_bytes=MIX_LIMIT),
        name="mix",
    )(early, late, halo, tw, gq, gk, gv)


def body(query_feat, key_feat, value_feat, grad_out, spatial_weight, temporal_weight):
    gq, gk, gv, early, late, halo = main_call(query_feat, key_feat, value_feat, grad_out, spatial_weight)
    gq, gk, gv, mixed = mix(early, late, halo, temporal_weight, gq, gk, gv)
    mixed = jnp.transpose(mixed.reshape(ROWS, 5, FRAMES, STRIPS * HEADS * D), (2, 0, 1, 3))
    return gq, gk, gv, mixed


def solution(mesh):
    wide = P("head", "seg")
    in_specs = (wide, wide, wide, wide, P(), P())
    out_specs = (wide, wide, wide, P("seg", None, "head", None))
    return jax.shard_map(body, mesh=mesh, in_specs=in_specs, out_specs=out_specs, check_vma=False)
```

```python
import functools

import jax
import jax.numpy as jnp
from jax import lax
from jax.experimental import pallas as pl
from jax.experimental.pallas import tpu as pltpu
from jax.sharding import PartitionSpec as P

D = 112
ROWS = 20
COLS = 40
FRAMES = 4
STRIDE = 768
WIN = 896
HEADS = 2
STRIPS = 8
CELLS = 100
SPLIT = 80
PACKED = SPLIT + CELLS
CHUNKS = ((0, 256), (256, 256), (512, 256), (768, 128))
BASE = 136
MESH = pl.DeviceIdType.MESH
F32 = jnp.float32
BF16 = jnp.bfloat16
MAIN_LIMIT = 39 << 20
MIX_LIMIT = 39 << 20


def split(x):
    hi = x.astype(BF16)
    lo = (x - hi.astype(F32)).astype(BF16)
    return hi, lo


def nn(a, b):
    return lax.dot_general(a, b, (((1,), (0,)), ((), ())), preferred_element_type=F32)


def nt(a, b):
    return lax.dot_general(a, b, (((1,), (1,)), ((), ())), preferred_element_type=F32)


def pad_rows(x):
    return jnp.concatenate([x, jnp.zeros((16, x.shape[1]), x.dtype)], axis=0)


def left_mul(pair, b_hi, b_lo):
    return nn(pair, jnp.concatenate([b_hi, b_hi], axis=0)) + nn(pair[:, :128], b_lo)


def outer(a_hi, a_lo, b_hi, b_lo):
    both = nt(jnp.concatenate([a_hi, a_lo], axis=0), b_hi)
    rows = a_hi.shape[0]
    return both[:rows] + both[rows:] + nt(a_hi, b_lo)


def in_frame(frame, start, width):
    lane = lax.broadcasted_iota(jnp.int32, (1, width), 1) + start
    return (lane >= 32 * frame) & (lane < 32 * frame + ROWS * COLS)


def extra_row(row):
    place = lax.broadcasted_iota(jnp.int32, (16, row.shape[1]), 0)
    return jnp.where(place == 0, jnp.broadcast_to(row, (16, row.shape[1])), 0.0)


def side_by_side(x):
    hi, lo = split(x)
    return jnp.concatenate([hi, lo], axis=1)


def greet(devices):
    barrier = pltpu.get_barrier_semaphore()
    for dev in devices:
        pl.semaphore_signal(barrier, inc=1, device_id=dev, device_id_type=MESH)
    pl.semaphore_wait(barrier, len(devices))


SEGS = 16
PIECE = 16
SCAN_SCRATCH = [
    pltpu.VMEM((SEGS, PIECE, 128), F32),
    pltpu.VMEM((SEGS, PIECE, 128), F32),
    pltpu.SemaphoreType.DMA((2, SEGS)),
    pltpu.SemaphoreType.DMA((2, SEGS)),
]


def seg_peers():
    seg, head = lax.axis_index("seg"), lax.axis_index("head")
    return [((seg + k) % SEGS, head) for k in range(1, SEGS)]


class Scan:
    def __init__(self, own, result, scratch, reverse):
        self.own, self.result, self.reverse = own, result, reverse
        self.got, self.back, self.send, self.recv = scratch
        self.seg = lax.axis_index("seg")
        self.peers = seg_peers()

    def copy(self, phase, k, src, dst):
        return pltpu.make_async_remote_copy(
            src_ref=src, dst_ref=dst, send_sem=self.send.at[phase, k], recv_sem=self.recv.at[phase, k],
            device_id=self.peers[k - 1], device_id_type=MESH,
        )

    def first(self):
        self.c1 = [
            self.copy(0, k, self.own.at[(self.seg + k) % SEGS], self.got.at[self.seg]) for k in range(1, SEGS)
        ]
        for c in self.c1:
            c.start()
        self.got[self.seg] = self.own[self.seg]

    def second(self):
        for c in self.c1:
            c.wait_recv()
        total = jnp.zeros((PIECE, 128), F32)
        order = range(SEGS - 1, -1, -1) if self.reverse else range(SEGS)
        for j in order:
            self.back[j] = total
            total = total + self.got[j]
        self.c2 = [
            self.copy(1, k, self.back.at[(self.seg + k) % SEGS], self.result.at[self.seg]) for k in range(1, SEGS)
        ]
        for c in self.c2:
            c.start()
        self.result[self.seg] = self.back[self.seg]

    def last(self):
        for c in self.c2:
            c.wait_recv()

    def drain(self):
        for c in self.c1 + self.c2:
            c.wait_send()


def ones_row(width):
    return extra_row(jnp.ones((1, width), F32)).astype(BF16)


def sums_frame(h, f, k_win, v_win):
    rows = slice(D * h, D * h + D)
    total = jnp.zeros((D, 128), F32)
    for start, width in CHUNKS:
        lanes = slice(start, start + width)
        ok = in_frame(f, start, width)
        k_hi, k_lo = split(jnp.where(ok, jnp.exp(k_win[f, rows, lanes]), 0.0))
        v_hi, v_lo = split(v_win[f, rows, lanes])
        v_hi = jnp.concatenate([v_hi, ones_row(width)], axis=0)
        total = total + outer(k_hi, k_lo, v_hi, pad_rows(v_lo))
    return total


def rows_of(ref, h):
    return jnp.concatenate([ref[7 * h + i] for i in range(7)], axis=0)


def put_rows(ref, h, value):
    for i in range(7):
        ref[7 * h + i] = value[PIECE * i:PIECE * i + PIECE]


def attend(f, q_win, state, att, inv):
    for h in range(HEADS):
        turned = side_by_side(pad_rows(state(h, f)).T)
        rows = slice(D * h, D * h + D)
        for start, width in CHUNKS:
            lanes = slice(start, start + width)
            q_hi, q_lo = split(jnp.exp(q_win[f, rows, lanes]))
            numer = left_mul(turned, pad_rows(q_hi), pad_rows(q_lo))
            inverse = 1.0 / numer[D:D + 1]
            att[f, rows, lanes] = jnp.where(in_frame(f, start, width), numer[:D] * inverse, 0.0)
            inv[f, h, 0:1, lanes] = inverse


def convolve(f, att, conv_in, w_own, send, rest):
    for m in range(WIN // 128):
        place = BASE - 32 * f + 128 * m
        conv_in[place:place + 128, :] = att[f, :, 128 * m:128 * m + 128].T
    edge = lax.broadcasted_iota(jnp.int32, (COLS, 128), 0)
    for lane in range(2):
        lanes = slice(128 * lane, 128 * lane + 128)
        taps = [[w_own[i, j:j + 1, lanes] for j in range(3)] for i in range(3)]
        for r in range(ROWS):
            lines = [conv_in[BASE + COLS * (r + i - 1):BASE + COLS * (r + i), lanes] for i in range(3)]
            cols = [taps[0][j] * lines[0] + taps[1][j] * lines[1] + taps[2][j] * lines[2] for j in range(3)]
            total = (
                cols[1]
                + jnp.where(edge == 0, 0.0, pltpu.roll(cols[0], 1, 0))
                + jnp.where(edge == COLS - 1, 0.0, pltpu.roll(cols[2], COLS - 1, 0))
            )
            half = 0.5 * total
            act = half + half * jnp.tanh(half)
            for j in range(STRIPS):
                part = act[5 * j:5 * j + 5]
                if lane == 0:
                    send[f, j, SPLIT + 5 * r:SPLIT + 5 * r + 5, :] = part
                elif 5 * r < SPLIT:
                    send[f, j, 5 * r:5 * r + 5, :] = part
                else:
                    rest[j, 5 * r - SPLIT:5 * r - SPLIT + 5, :] = part
    free = lax.broadcasted_iota(jnp.int32, (24, 128), 1) >= 96
    for j in range(STRIPS):
        for p in range(3):
            rows = slice(24 * p, 24 * p + 24)
            send[f, j, rows, :] = jnp.where(free, pltpu.roll(rest[j], 96 - 32 * p, 1), send[f, j, rows, :])


def place_of(f, start, width):
    return slice(STRIDE * f + start, STRIDE * f + start + width)


def query_grads(f, q_win, g_win, state, att, inv, gq_ref, ds):
    for h in range(HEADS):
        plain = side_by_side(state(h, f))
        rows = slice(D * h, D * h + D)
        grad_state = jnp.zeros((D, 128), F32)
        for start, width in CHUNKS:
            lanes = slice(start, start + width)
            ok = in_frame(f, start, width)
            feat = jnp.exp(q_win[f, rows, lanes])
            q_hi, q_lo = split(feat)
            inverse = inv[f, h, 0:1, lanes]
            grad = g_win[f, rows, lanes]
            slope = -jnp.sum(grad * att[f, rows, lanes], axis=0, keepdims=True) * inverse
            ext = jnp.where(ok, jnp.concatenate([grad * inverse, extra_row(slope)], axis=0), 0.0)
            n_hi, n_lo = split(ext)
            gq = left_mul(plain, n_hi, n_lo) * feat
            place = place_of(f, start, width)
            gq_ref[rows, place] = jnp.where(ok, gq, gq_ref[rows, place])
            grad_state = grad_state + outer(q_hi, q_lo, n_hi, n_lo)
        ds[h, f] = grad_state


def key_grads(f, k_win, v_win, state, gk_ref, gv_ref):
    for h in range(HEADS):
        plain = side_by_side(state(h, f))
        turned = side_by_side(pad_rows(state(h, f)).T)
        rows = slice(D * h, D * h + D)
        for start, width in CHUNKS:
            lanes = slice(start, start + width)
            ok = in_frame(f, start, width)
            feat = jnp.exp(k_win[f, rows, lanes])
            k_hi, k_lo = split(feat)
            v_hi, v_lo = split(v_win[f, rows, lanes])
            v_hi = jnp.concatenate([v_hi, ones_row(width)], axis=0)
            gk = left_mul(plain, v_hi, pad_rows(v_lo)) * feat
            gv = left_mul(turned, pad_rows(k_hi), pad_rows(k_lo))[:D]
            place = place_of(f, start, width)
            gk_ref[rows, place] = jnp.where(ok, gk, gk_ref[rows, place])
            gv_ref[rows, place] = jnp.where(ok, gv, gv_ref[rows, place])


ORDER = (2, 3, 0, 1)
HOPS = (1, 2, 6, 3, 5, 7, 4)
RELAYED = ((3, 0), (2, 1), (3, 1))


def main_kernel(q_ref, k_ref, v_ref, g_ref, sw_ref, gq_ref, gk_ref, gv_ref, got_early, got_late, halo_ref,
                q_win, k_win, v_win, g_win, att, inv, conv_in, act, rest, w_own, local, ds, own, before, after,
                load, send, recv, fsend, frecv, lsem, relay, rsend, rrecv, *scratch):
    seg, head = lax.axis_index("seg"), lax.axis_index("head")
    peers = [(seg, head ^ k) for k in range(1, 8)]
    up = ((seg + 1) % SEGS, head)
    barrier = pltpu.get_barrier_semaphore()
    for dev in seg_peers() + peers:
        pl.semaphore_signal(barrier, inc=1, device_id=dev, device_id_type=MESH)

    wins = ((k_ref, k_win), (v_ref, v_win), (q_ref, q_win), (g_ref, g_win))

    def loading(i, f):
        src, dst = wins[i]
        return pltpu.make_async_copy(src.at[:, STRIDE * f:STRIDE * f + WIN], dst.at[f], load.at[i, f])

    for f in range(FRAMES):
        for i in range(2):
            loading(i, f).start()

    def got_at(k, f):
        return (got_early if f >= 2 else got_late).at[k, f % 2]

    def strip(f, k):
        return pltpu.make_async_remote_copy(
            src_ref=act.at[f, head ^ k], dst_ref=got_at(k, f), send_sem=send.at[f, k], recv_sem=recv.at[f, k],
            device_id=(seg, head ^ k), device_id_type=MESH,
        )

    def forward(f, k):
        src = act.at[f, head] if k == 0 else got_at(k, f)
        return pltpu.make_async_remote_copy(
            src_ref=src, dst_ref=halo_ref.at[k, f - 2], send_sem=fsend.at[f - 2, k], recv_sem=frecv.at[f - 2, k],
            device_id=up, device_id_type=MESH,
        )

    def mine(f):
        return pltpu.make_async_copy(act.at[f, head], got_at(0, f), lsem.at[f])

    x, y = seg // 4, seg % 4
    below = (4 * x + (y + 3) % 4, head)
    beyond = ((4 * x + (y + 2) % 4 + 1) % SEGS, head)

    def detour(leg, i):
        f, k = RELAYED[i]
        if leg == 0:
            src = act.at[f, head] if k == 0 else got_at(k, f)
        else:
            src = relay.at[leg - 1, i]
        dst, sem = (halo_ref.at[k, f - 2], frecv.at[f - 2, k]) if leg == 2 else (relay.at[leg, i], rrecv.at[leg, i])
        return pltpu.make_async_remote_copy(
            src_ref=src, dst_ref=dst, send_sem=rsend.at[leg, i], recv_sem=sem,
            device_id=beyond if leg == 2 else below, device_id_type=MESH,
        )

    def take_detour(leg, i):
        f, k = RELAYED[i]
        if leg == 0 and k:
            strip(f, k).wait_recv()

        @pl.when(seg != SEGS - 1 - leg)
        def _():
            if leg:
                detour(leg - 1, i).wait_recv()
            detour(leg, i).start()

    queue = [(2, 0)] + [(2, k) for k in HOPS[1:]] + [(3, k) for k in HOPS[1:]]

    def pass_on(count):
        for f, k in queue[:count]:
            if k:
                strip(f, k).wait_recv()

            @pl.when(seg != SEGS - 1)
            def _():
                forward(f, k).start()
        del queue[:count]

    for p in (SEGS - 2, SEGS - 1):
        own[p] = jnp.zeros((PIECE, 128), F32)

    for f in range(FRAMES):
        loading(0, f).wait()
        loading(1, f).wait()
        for h in range(HEADS):
            local[h, f] = sums_frame(h, f, k_win, v_win)
    for h in range(HEADS):
        for f in range(1, FRAMES):
            local[h, f] = local[h, f] + local[h, f - 1]
        put_rows(own, h, local[h, FRAMES - 1])
    pl.semaphore_wait(barrier, SEGS - 1 + 7)
    scan = Scan(own, before, scratch[:4], False)
    scan.first()
    for i in (2, 3):
        for f in ORDER:
            loading(i, f).start()
    lanes = pl.ds(0, 256)
    chans = HEADS * D
    for i in range(3):
        taps = sw_ref[i, :, :256]
        for o in range(1, STRIPS):
            begin = min(chans * o, STRIPS * chans - 256)
            part = sw_ref[i, :, begin:begin + 256]
            if begin < chans * o:
                part = pltpu.roll(part, 256 - (chans * o - begin), 1)
            taps = jnp.where(head == o, part, taps)
        w_own[i, 0:3] = taps
    for f in range(FRAMES):
        att[f, HEADS * D:, :] = jnp.zeros((32, WIN), F32)
    conv_in[BASE + 800:, :] = jnp.zeros((WIN - 800, 256), F32)
    scan.second()
    scan.last()

    def state(h, f):
        return rows_of(before, h) + local[h, f]

    for i, f in enumerate(ORDER):
        loading(2, f).wait()
        attend(f, q_win, state, att, inv)
        convolve(f, att, conv_in, w_own, act, rest)
        for k in HOPS:
            strip(f, k).start()
        mine(f).start()
        pass_on((1, 0, 2, 2)[i])
        if i == 1:
            take_detour(0, 0)
            take_detour(0, 1)
        if i == 2:
            take_detour(0, 2)
    for i, f in enumerate(ORDER):
        loading(3, f).wait()
        query_grads(f, q_win, g_win, state, att, inv, gq_ref, ds)
    scan.drain()
    for h in range(HEADS):
        for f in range(FRAMES - 2, -1, -1):
            ds[h, f] = ds[h, f] + ds[h, f + 1]
        put_rows(own, h, ds[h, 0])
    scan = Scan(own, after, scratch[4:], True)
    scan.first()
    pass_on(2)
    for i in range(3):
        take_detour(1, i)
    pass_on(2)
    scan.second()
    pass_on(2)
    for i in range(3):
        take_detour(2, i)
    pass_on(1)
    scan.last()

    def later(h, f):
        return rows_of(after, h) + ds[h, f]

    for f in range(FRAMES):
        key_grads(f, k_win, v_win, later, gk_ref, gv_ref)
        pass_on(1)
    pass_on(len(queue))
    scan.drain()
    for f in range(FRAMES):
        mine(f).wait()
    for f in (0, 1):
        for k in HOPS:
            strip(f, k).wait_recv()
    for f in ORDER:
        for k in HOPS:
            strip(f, k).wait_send()
    for f in (2, 3):
        for k in (0,) + HOPS:
            if (f, k) in RELAYED:
                i = RELAYED.index((f, k))
                for leg in range(3):
                    pl.when(seg != SEGS - 1 - leg)(detour(leg, i).wait_send)
                pl.when(seg != 0)(detour(2, i).wait_recv)
            else:
                pl.when(seg != SEGS - 1)(forward(f, k).wait_send)
                pl.when(seg != 0)(forward(f, k).wait_recv)


def main_call(q, k, v, g, weights):
    hbm = pl.BlockSpec(memory_space=pl.ANY)
    vmem = pl.BlockSpec(memory_space=pltpu.VMEM)
    wide = jax.ShapeDtypeStruct((HEADS * D, STRIDE * 3 + WIN), F32)
    half = jax.ShapeDtypeStruct((STRIPS, 2, PACKED, 128), F32)
    window = pltpu.VMEM((FRAMES, HEADS * D, WIN), F32)
    states = pltpu.VMEM((HEADS, FRAMES, D, 128), F32)
    pieces = pltpu.VMEM((SEGS, PIECE, 128), F32)
    return pl.pallas_call(
        main_kernel,
        out_shape=(
            wide,
            wide,
            wide,
            half,
            half,
            half,
        ),
        in_specs=[hbm] * 4 + [vmem],
        out_specs=(vmem, vmem, vmem, hbm, hbm, hbm),
        scratch_shapes=[
            window, window, window, window,
            pltpu.VMEM((FRAMES, 256, WIN), F32),
            pltpu.VMEM((FRAMES, HEADS, 8, WIN), F32),
            pltpu.VMEM((BASE + WIN, 256), F32),
            pltpu.VMEM((FRAMES, STRIPS, PACKED, 128), F32),
            pltpu.VMEM((STRIPS, 24, 128), F32),
            pltpu.VMEM((3, 8, 256), F32),
            states, states, pieces, pieces, pieces,
            pltpu.SemaphoreType.DMA((4, FRAMES)),
            pltpu.SemaphoreType.DMA((FRAMES, 8)),
            pltpu.SemaphoreType.DMA((FRAMES, 8)),
            pltpu.SemaphoreType.DMA((2, 8)),
            pltpu.SemaphoreType.DMA((2, 8)),
            pltpu.SemaphoreType.DMA((FRAMES,)),
            pltpu.VMEM((2, 3, PACKED, 128), F32),
            pltpu.SemaphoreType.DMA((3, 3)),
            pltpu.SemaphoreType.DMA((2, 3)),
        ] + SCAN_SCRATCH + SCAN_SCRATCH,
        compiler_params=pltpu.CompilerParams(collective_id=0, has_side_effects=True, vmem_limit_bytes=MAIN_LIMIT),
        name="attention_exchange",
    )(q, k, v, g, weights)


def cells(ref, index, base, count, lane):
    if lane == 0:
        return ref[index + (pl.ds(SPLIT + base, count),)]
    if not isinstance(base, int):
        return ref[index + (pl.ds(base, count),)]
    place = lax.broadcasted_iota(jnp.int32, (count, 128), 1)
    parts = [
        pltpu.roll(ref[index + (slice(24 * p + base - SPLIT, 24 * p + base - SPLIT + count),)], 32 + 32 * p, 1)
        for p in range(3)
    ]
    return jnp.where(place < 32, parts[0], jnp.where(place < 64, parts[1], parts[2]))


def mix_group(base, count, halo_on, got, halo, tw_ref, tmp):
    head = lax.axis_index("head")
    place = lax.broadcasted_iota(jnp.int32, (count, 128), 1)
    pending = [None] * FRAMES
    for owner in range(STRIPS):
        slot = head ^ owner
        for lane in range(2):
            acts = [jnp.where(halo_on, cells(halo, (slot, i), base, count, lane), 0.0) for i in range(2)]
            acts += [cells(got[f // 2], (slot, f % 2), base, count, lane) for f in range(FRAMES)]
            w = [tw_ref[owner, i:i + 1, 128 * lane:128 * lane + 128] for i in range(3)]
            width = 128 if lane == 0 else 96
            tile, shift = divmod(224 * owner + 128 * lane, 128)
            for f in range(FRAMES):
                val = w[0] * acts[f + 2] + w[1] * acts[f + 1] + w[2] * acts[f]
                full = val
                if shift:
                    val = pltpu.roll(val, shift, 1)
                    full = jnp.where(place < shift, pending[f], val)
                if shift + width >= 128:
                    tmp[tile, pl.ds(f, count, stride=4), :] = full
                    pending[f] = val
                else:
                    pending[f] = full


def mix_kernel(got_early, got_late, halo, tw_ref, gq, gk, gv, gq_out, gk_out, gv_out, mixed_out, tmp, tw, mixed, sem, msem):
    plain = [
        pltpu.make_async_copy(src, dst, sem.at[i])
        for i, (src, dst) in enumerate(((gq, gq_out), (gk, gk_out), (gv, gv_out)))
    ]
    for c in plain:
        c.start()
    for owner in range(STRIPS):
        begin = min(224 * owner, 1792 - 256)
        part = tw_ref[:, begin:begin + 256]
        if begin < 224 * owner:
            part = pltpu.roll(part, 256 - (224 * owner - begin), 1)
        tw[owner, 0:3] = part
    halo_on = lax.axis_index("seg") > 0

    def leaving(base, count, i):
        rows = pl.ds(base, count)
        return pltpu.make_async_copy(mixed.at[rows], mixed_out.at[rows], msem.at[i])

    def group(base, count, g):
        mix_group(base, count, halo_on, (got_late, got_early), halo, tw, tmp)
        for i in range(count):
            for t in range(14):
                mixed[base + i, :, 128 * t:128 * t + 128] = tmp[t, 4 * i:4 * i + 4, :]
        leaving(base, count, g).start()

    def step(i, carry):
        group(pl.multiple_of(8 * i, 8), 8, i)
        return carry

    lax.fori_loop(0, 10, step, 0)
    group(80, 8, 10)
    group(88, 8, 11)
    group(96, 4, 12)
    for g in range(13):
        leaving(8 * g, 4 if g == 12 else 8, g).wait()
    for c in plain:
        c.wait()


def mix(early, late, halo, tw, gq, gk, gv):
    vmem = pl.BlockSpec(memory_space=pltpu.VMEM)
    hbm = pl.BlockSpec(memory_space=pl.ANY)
    wide = jax.ShapeDtypeStruct(gq.shape, F32)
    return pl.pallas_call(
        mix_kernel,
        out_shape=(wide, wide, wide, jax.ShapeDtypeStruct((CELLS, FRAMES, 1792), F32)),
        in_specs=[vmem] * 7,
        out_specs=(hbm, hbm, hbm, hbm),
        scratch_shapes=[
            pltpu.VMEM((14, 32, 128), F32),
            pltpu.VMEM((STRIPS, 8, 256), F32),
            pltpu.VMEM((CELLS, FRAMES, 1792), F32),
            pltpu.SemaphoreType.DMA((3,)),
            pltpu.SemaphoreType.DMA((13,)),
        ],
        compiler_params=pltpu.CompilerParams(vmem_limit_bytes=MIX_LIMIT),
        name="mix",
    )(early, late, halo, tw, gq, gk, gv)


def body(query_feat, key_feat, value_feat, grad_out, spatial_weight, temporal_weight):
    gq, gk, gv, early, late, halo = main_call(query_feat, key_feat, value_feat, grad_out, spatial_weight)
    gq, gk, gv, mixed = mix(early, late, halo, temporal_weight, gq, gk, gv)
    mixed = jnp.transpose(mixed.reshape(ROWS, 5, FRAMES, STRIPS * HEADS * D), (2, 0, 1, 3))
    return gq, gk, gv, mixed


def solution(mesh):
    wide = P("head", "seg")
    in_specs = (wide, wide, wide, wide, P(), P())
    out_specs = (wide, wide, wide, P("seg", None, "head", None))
    return jax.shard_map(body, mesh=mesh, in_specs=in_specs, out_specs=out_specs, check_vma=False)
```

```python
import functools

import jax
import jax.numpy as jnp
from jax import lax
from jax.experimental import pallas as pl
from jax.experimental.pallas import tpu as pltpu
from jax.sharding import PartitionSpec as P

D = 112
ROWS = 20
COLS = 40
FRAMES = 4
STRIDE = 768
WIN = 896
HEADS = 2
STRIPS = 8
CELLS = 100
SECOND = 104
PLAIN = 72
REST = 76
PACKED = SECOND + PLAIN
CHUNKS = ((0, 256), (256, 256), (512, 256), (768, 128))
BASE = 136
MESH = pl.DeviceIdType.MESH
F32 = jnp.float32
BF16 = jnp.bfloat16
MAIN_LIMIT = 39 << 20
MIX_LIMIT = 39 << 20


def split(x):
    hi = x.astype(BF16)
    lo = (x - hi.astype(F32)).astype(BF16)
    return hi, lo


def nn(a, b):
    return lax.dot_general(a, b, (((1,), (0,)), ((), ())), preferred_element_type=F32)


def nt(a, b):
    return lax.dot_general(a, b, (((1,), (1,)), ((), ())), preferred_element_type=F32)


def pad_rows(x):
    return jnp.concatenate([x, jnp.zeros((16, x.shape[1]), x.dtype)], axis=0)


def left_mul(pair, b_hi, b_lo):
    return nn(pair, jnp.concatenate([b_hi, b_hi], axis=0)) + nn(pair[:, :128], b_lo)


def outer(a_hi, a_lo, b_hi, b_lo):
    both = nt(jnp.concatenate([a_hi, a_lo], axis=0), b_hi)
    rows = a_hi.shape[0]
    return both[:rows] + both[rows:] + nt(a_hi, b_lo)


def in_frame(frame, start, width):
    lane = lax.broadcasted_iota(jnp.int32, (1, width), 1) + start
    return (lane >= 32 * frame) & (lane < 32 * frame + ROWS * COLS)


def extra_row(row):
    place = lax.broadcasted_iota(jnp.int32, (16, row.shape[1]), 0)
    return jnp.where(place == 0, jnp.broadcast_to(row, (16, row.shape[1])), 0.0)


def side_by_side(x):
    hi, lo = split(x)
    return jnp.concatenate([hi, lo], axis=1)


def greet(devices):
    barrier = pltpu.get_barrier_semaphore()
    for dev in devices:
        pl.semaphore_signal(barrier, inc=1, device_id=dev, device_id_type=MESH)
    pl.semaphore_wait(barrier, len(devices))


SEGS = 16
PIECE = 16
SCAN_SCRATCH = [
    pltpu.VMEM((SEGS, PIECE, 128), F32),
    pltpu.VMEM((SEGS, PIECE, 128), F32),
    pltpu.SemaphoreType.DMA((2, SEGS)),
    pltpu.SemaphoreType.DMA((2, SEGS)),
]


def seg_peers():
    seg, head = lax.axis_index("seg"), lax.axis_index("head")
    return [((seg + k) % SEGS, head) for k in range(1, SEGS)]


class Scan:
    def __init__(self, own, result, scratch, reverse):
        self.own, self.result, self.reverse = own, result, reverse
        self.got, self.back, self.send, self.recv = scratch
        self.seg = lax.axis_index("seg")
        self.peers = seg_peers()

    def copy(self, phase, k, src, dst):
        return pltpu.make_async_remote_copy(
            src_ref=src, dst_ref=dst, send_sem=self.send.at[phase, k], recv_sem=self.recv.at[phase, k],
            device_id=self.peers[k - 1], device_id_type=MESH,
        )

    def first(self):
        self.c1 = [
            self.copy(0, k, self.own.at[(self.seg + k) % SEGS], self.got.at[self.seg]) for k in range(1, SEGS)
        ]
        for c in self.c1:
            c.start()
        self.got[self.seg] = self.own[self.seg]

    def second(self):
        for c in self.c1:
            c.wait_recv()
        total = jnp.zeros((PIECE, 128), F32)
        order = range(SEGS - 1, -1, -1) if self.reverse else range(SEGS)
        for j in order:
            self.back[j] = total
            total = total + self.got[j]
        self.c2 = [
            self.copy(1, k, self.back.at[(self.seg + k) % SEGS], self.result.at[self.seg]) for k in range(1, SEGS)
        ]
        for c in self.c2:
            c.start()
        self.result[self.seg] = self.back[self.seg]

    def last(self):
        for c in self.c2:
            c.wait_recv()

    def drain(self):
        for c in self.c1 + self.c2:
            c.wait_send()


def ones_row(width):
    return extra_row(jnp.ones((1, width), F32)).astype(BF16)


def sums_frame(h, f, k_win, v_win):
    rows = slice(D * h, D * h + D)
    total = jnp.zeros((D, 128), F32)
    for start, width in CHUNKS:
        lanes = slice(start, start + width)
        ok = in_frame(f, start, width)
        k_hi, k_lo = split(jnp.where(ok, jnp.exp(k_win[f, rows, lanes]), 0.0))
        v_hi, v_lo = split(v_win[f, rows, lanes])
        v_hi = jnp.concatenate([v_hi, ones_row(width)], axis=0)
        total = total + outer(k_hi, k_lo, v_hi, pad_rows(v_lo))
    return total


def rows_of(ref, h):
    return jnp.concatenate([ref[7 * h + i] for i in range(7)], axis=0)


def put_rows(ref, h, value):
    for i in range(7):
        ref[7 * h + i] = value[PIECE * i:PIECE * i + PIECE]


def attend(f, q_win, state, att, inv):
    for h in range(HEADS):
        turned = side_by_side(pad_rows(state(h, f)).T)
        rows = slice(D * h, D * h + D)
        for start, width in CHUNKS:
            lanes = slice(start, start + width)
            q_hi, q_lo = split(jnp.exp(q_win[f, rows, lanes]))
            numer = left_mul(turned, pad_rows(q_hi), pad_rows(q_lo))
            inverse = 1.0 / numer[D:D + 1]
            att[f, rows, lanes] = jnp.where(in_frame(f, start, width), numer[:D] * inverse, 0.0)
            inv[f, h, 0:1, lanes] = inverse


def convolve(f, att, conv_in, w_own, send, rest):
    for m in range(WIN // 128):
        place = BASE - 32 * f + 128 * m
        conv_in[place:place + 128, :] = att[f, :, 128 * m:128 * m + 128].T
    edge = lax.broadcasted_iota(jnp.int32, (COLS, 128), 0)
    for lane in range(2):
        lanes = slice(128 * lane, 128 * lane + 128)
        taps = [[w_own[i, j:j + 1, lanes] for j in range(3)] for i in range(3)]
        for r in range(ROWS):
            lines = [conv_in[BASE + COLS * (r + i - 1):BASE + COLS * (r + i), lanes] for i in range(3)]
            cols = [taps[0][j] * lines[0] + taps[1][j] * lines[1] + taps[2][j] * lines[2] for j in range(3)]
            total = (
                cols[1]
                + jnp.where(edge == 0, 0.0, pltpu.roll(cols[0], 1, 0))
                + jnp.where(edge == COLS - 1, 0.0, pltpu.roll(cols[2], COLS - 1, 0))
            )
            half = 0.5 * total
            act = half + half * jnp.tanh(half)
            for j in range(STRIPS):
                part = act[5 * j:5 * j + 5]
                if lane == 0:
                    send[f, j, 5 * r:5 * r + 5, :] = part
                    continue
                for low, high, to in ((0, PLAIN, SECOND), (PLAIN, REST, CELLS), (REST, CELLS, None)):
                    a, b = max(5 * r, low), min(5 * r + 5, high)
                    if a < b and to is None:
                        rest[j, a - REST:b - REST, :] = part[a - 5 * r:b - 5 * r]
                    elif a < b:
                        send[f, j, to + a - low:to + b - low, :] = part[a - 5 * r:b - 5 * r]
    free = lax.broadcasted_iota(jnp.int32, (24, 128), 1) >= 96
    for j in range(STRIPS):
        for p in range(3):
            rows = slice(SECOND + 24 * p, SECOND + 24 * p + 24)
            send[f, j, rows, :] = jnp.where(free, pltpu.roll(rest[j], 96 - 32 * p, 1), send[f, j, rows, :])


def place_of(f, start, width):
    return slice(STRIDE * f + start, STRIDE * f + start + width)


def query_grads(f, q_win, g_win, state, att, inv, gq_ref, ds):
    for h in range(HEADS):
        plain = side_by_side(state(h, f))
        rows = slice(D * h, D * h + D)
        grad_state = jnp.zeros((D, 128), F32)
        for start, width in CHUNKS:
            lanes = slice(start, start + width)
            ok = in_frame(f, start, width)
            feat = jnp.exp(q_win[f, rows, lanes])
            q_hi, q_lo = split(feat)
            inverse = inv[f, h, 0:1, lanes]
            grad = g_win[f, rows, lanes]
            slope = -jnp.sum(grad * att[f, rows, lanes], axis=0, keepdims=True) * inverse
            ext = jnp.where(ok, jnp.concatenate([grad * inverse, extra_row(slope)], axis=0), 0.0)
            n_hi, n_lo = split(ext)
            gq = left_mul(plain, n_hi, n_lo) * feat
            place = place_of(f, start, width)
            gq_ref[rows, place] = jnp.where(ok, gq, gq_ref[rows, place])
            grad_state = grad_state + outer(q_hi, q_lo, n_hi, n_lo)
        ds[h, f] = grad_state


def key_grads(f, k_win, v_win, state, gk_ref, gv_ref):
    for h in range(HEADS):
        plain = side_by_side(state(h, f))
        turned = side_by_side(pad_rows(state(h, f)).T)
        rows = slice(D * h, D * h + D)
        for start, width in CHUNKS:
            lanes = slice(start, start + width)
            ok = in_frame(f, start, width)
            feat = jnp.exp(k_win[f, rows, lanes])
            k_hi, k_lo = split(feat)
            v_hi, v_lo = split(v_win[f, rows, lanes])
            v_hi = jnp.concatenate([v_hi, ones_row(width)], axis=0)
            gk = left_mul(plain, v_hi, pad_rows(v_lo)) * feat
            gv = left_mul(turned, pad_rows(k_hi), pad_rows(k_lo))[:D]
            place = place_of(f, start, width)
            gk_ref[rows, place] = jnp.where(ok, gk, gk_ref[rows, place])
            gv_ref[rows, place] = jnp.where(ok, gv, gv_ref[rows, place])


ORDER = (2, 3, 0, 1)
HOPS = (1, 2, 6, 3, 5, 7, 4)
FAR_FIRST = (4, 5, 2, 6, 3, 7, 1)
RELAYED = ((3, 0), (2, 1), (3, 1))


def main_kernel(q_ref, k_ref, v_ref, g_ref, sw_ref, gq_ref, gk_ref, gv_ref, got_early, got_late, halo_ref,
                q_win, k_win, v_win, g_win, att, inv, conv_in, act, rest, w_own, local, ds, own, before, after,
                load, send, recv, fsend, frecv, lsem, relay, rsend, rrecv, *scratch):
    seg, head = lax.axis_index("seg"), lax.axis_index("head")
    peers = [(seg, head ^ k) for k in range(1, 8)]
    up = ((seg + 1) % SEGS, head)
    barrier = pltpu.get_barrier_semaphore()
    for dev in seg_peers() + peers:
        pl.semaphore_signal(barrier, inc=1, device_id=dev, device_id_type=MESH)

    wins = ((k_ref, k_win), (v_ref, v_win), (q_ref, q_win), (g_ref, g_win))

    def loading(i, f):
        src, dst = wins[i]
        return pltpu.make_async_copy(src.at[:, STRIDE * f:STRIDE * f + WIN], dst.at[f], load.at[i, f])

    for f in range(FRAMES):
        for i in range(2):
            loading(i, f).start()

    def got_at(k, f):
        return (got_early if f >= 2 else got_late).at[k, f % 2]

    def strip(f, k):
        return pltpu.make_async_remote_copy(
            src_ref=act.at[f, head ^ k], dst_ref=got_at(k, f), send_sem=send.at[f, k], recv_sem=recv.at[f, k],
            device_id=(seg, head ^ k), device_id_type=MESH,
        )

    def forward(f, k):
        src = act.at[f, head] if k == 0 else got_at(k, f)
        return pltpu.make_async_remote_copy(
            src_ref=src, dst_ref=halo_ref.at[k, f - 2], send_sem=fsend.at[f - 2, k], recv_sem=frecv.at[f - 2, k],
            device_id=up, device_id_type=MESH,
        )

    def mine(f):
        return pltpu.make_async_copy(act.at[f, head], got_at(0, f), lsem.at[f])

    x, y = seg // 4, seg % 4
    below = (4 * x + (y + 3) % 4, head)
    beyond = ((4 * x + (y + 2) % 4 + 1) % SEGS, head)

    def detour(leg, i):
        f, k = RELAYED[i]
        if leg == 0:
            src = act.at[f, head] if k == 0 else got_at(k, f)
        else:
            src = relay.at[leg - 1, i]
        dst, sem = (halo_ref.at[k, f - 2], frecv.at[f - 2, k]) if leg == 2 else (relay.at[leg, i], rrecv.at[leg, i])
        return pltpu.make_async_remote_copy(
            src_ref=src, dst_ref=dst, send_sem=rsend.at[leg, i], recv_sem=sem,
            device_id=beyond if leg == 2 else below, device_id_type=MESH,
        )

    def take_detour(leg, i):
        f, k = RELAYED[i]
        if leg == 0 and k:
            strip(f, k).wait_recv()

        @pl.when(seg != SEGS - 1 - leg)
        def _():
            if leg:
                detour(leg - 1, i).wait_recv()
            detour(leg, i).start()

    queue = [(2, 0)] + [(2, k) for k in HOPS[1:]] + [(3, k) for k in HOPS[1:]]

    def pass_on(count):
        for f, k in queue[:count]:
            if k:
                strip(f, k).wait_recv()

            @pl.when(seg != SEGS - 1)
            def _():
                forward(f, k).start()
        del queue[:count]

    for p in (SEGS - 2, SEGS - 1):
        own[p] = jnp.zeros((PIECE, 128), F32)

    for f in range(FRAMES):
        loading(0, f).wait()
        loading(1, f).wait()
        for h in range(HEADS):
            local[h, f] = sums_frame(h, f, k_win, v_win)
    for h in range(HEADS):
        for f in range(1, FRAMES):
            local[h, f] = local[h, f] + local[h, f - 1]
        put_rows(own, h, local[h, FRAMES - 1])
    pl.semaphore_wait(barrier, SEGS - 1 + 7)
    scan = Scan(own, before, scratch[:4], False)
    scan.first()
    for i in (2, 3):
        for f in ORDER:
            loading(i, f).start()
    lanes = pl.ds(0, 256)
    chans = HEADS * D
    for i in range(3):
        taps = sw_ref[i, :, :256]
        for o in range(1, STRIPS):
            begin = min(chans * o, STRIPS * chans - 256)
            part = sw_ref[i, :, begin:begin + 256]
            if begin < chans * o:
                part = pltpu.roll(part, 256 - (chans * o - begin), 1)
            taps = jnp.where(head == o, part, taps)
        w_own[i, 0:3] = taps
    for f in range(FRAMES):
        att[f, HEADS * D:, :] = jnp.zeros((32, WIN), F32)
    conv_in[BASE + 800:, :] = jnp.zeros((WIN - 800, 256), F32)
    scan.second()
    scan.last()

    def state(h, f):
        return rows_of(before, h) + local[h, f]

    for i, f in enumerate(ORDER):
        loading(2, f).wait()
        attend(f, q_win, state, att, inv)
        convolve(f, att, conv_in, w_own, act, rest)
        for k in HOPS if f >= 2 else FAR_FIRST:
            strip(f, k).start()
        mine(f).start()
        pass_on((1, 0, 2, 2)[i])
        if i == 1:
            take_detour(0, 0)
            take_detour(0, 1)
        if i == 2:
            take_detour(0, 2)
    for i, f in enumerate(ORDER):
        loading(3, f).wait()
        query_grads(f, q_win, g_win, state, att, inv, gq_ref, ds)
    scan.drain()
    for h in range(HEADS):
        for f in range(FRAMES - 2, -1, -1):
            ds[h, f] = ds[h, f] + ds[h, f + 1]
        put_rows(own, h, ds[h, 0])
    scan = Scan(own, after, scratch[4:], True)
    scan.first()
    pass_on(2)
    for i in range(3):
        take_detour(1, i)
    pass_on(2)
    scan.second()
    pass_on(2)
    for i in range(3):
        take_detour(2, i)
    pass_on(1)
    scan.last()

    def later(h, f):
        return rows_of(after, h) + ds[h, f]

    for f in range(FRAMES):
        key_grads(f, k_win, v_win, later, gk_ref, gv_ref)
        pass_on(1)
    pass_on(len(queue))
    scan.drain()
    for f in range(FRAMES):
        mine(f).wait()
    for f in (0, 1):
        for k in HOPS:
            strip(f, k).wait_recv()
    for f in ORDER:
        for k in HOPS:
            strip(f, k).wait_send()
    for f in (2, 3):
        for k in (0,) + HOPS:
            if (f, k) in RELAYED:
                i = RELAYED.index((f, k))
                for leg in range(3):
                    pl.when(seg != SEGS - 1 - leg)(detour(leg, i).wait_send)
                pl.when(seg != 0)(detour(2, i).wait_recv)
            else:
                pl.when(seg != SEGS - 1)(forward(f, k).wait_send)
                pl.when(seg != 0)(forward(f, k).wait_recv)


def main_call(q, k, v, g, weights):
    hbm = pl.BlockSpec(memory_space=pl.ANY)
    vmem = pl.BlockSpec(memory_space=pltpu.VMEM)
    wide = jax.ShapeDtypeStruct((HEADS * D, STRIDE * 3 + WIN), F32)
    half = jax.ShapeDtypeStruct((STRIPS, 2, PACKED, 128), F32)
    window = pltpu.VMEM((FRAMES, HEADS * D, WIN), F32)
    states = pltpu.VMEM((HEADS, FRAMES, D, 128), F32)
    pieces = pltpu.VMEM((SEGS, PIECE, 128), F32)
    return pl.pallas_call(
        main_kernel,
        out_shape=(
            wide,
            wide,
            wide,
            half,
            half,
            half,
        ),
        in_specs=[hbm] * 4 + [vmem],
        out_specs=(vmem, vmem, vmem, hbm, hbm, hbm),
        scratch_shapes=[
            window, window, window, window,
            pltpu.VMEM((FRAMES, 256, WIN), F32),
            pltpu.VMEM((FRAMES, HEADS, 8, WIN), F32),
            pltpu.VMEM((BASE + WIN, 256), F32),
            pltpu.VMEM((FRAMES, STRIPS, PACKED, 128), F32),
            pltpu.VMEM((STRIPS, 24, 128), F32),
            pltpu.VMEM((3, 8, 256), F32),
            states, states, pieces, pieces, pieces,
            pltpu.SemaphoreType.DMA((4, FRAMES)),
            pltpu.SemaphoreType.DMA((FRAMES, 8)),
            pltpu.SemaphoreType.DMA((FRAMES, 8)),
            pltpu.SemaphoreType.DMA((2, 8)),
            pltpu.SemaphoreType.DMA((2, 8)),
            pltpu.SemaphoreType.DMA((FRAMES,)),
            pltpu.VMEM((2, 3, PACKED, 128), F32),
            pltpu.SemaphoreType.DMA((3, 3)),
            pltpu.SemaphoreType.DMA((2, 3)),
        ] + SCAN_SCRATCH + SCAN_SCRATCH,
        compiler_params=pltpu.CompilerParams(collective_id=0, has_side_effects=True, vmem_limit_bytes=MAIN_LIMIT),
        name="attention_exchange",
    )(q, k, v, g, weights)


def cells(ref, index, base, count, lane):
    if lane == 0:
        return ref[index + (pl.ds(base, count),)]
    if not isinstance(base, int):
        return ref[index + (pl.ds(SECOND + base, count),)]
    place = lax.broadcasted_iota(jnp.int32, (count, 128), 1)
    begin = max(base - REST, -4)
    parts = [
        pltpu.roll(ref[index + (slice(SECOND + 24 * p + begin, SECOND + 24 * p + begin + count),)], 32 + 32 * p, 1)
        for p in range(3)
    ]
    value = jnp.where(place < 32, parts[0], jnp.where(place < 64, parts[1], parts[2]))
    if begin < 0:
        row = lax.broadcasted_iota(jnp.int32, (count, 128), 0)
        value = jnp.where(row < 4, ref[index + (slice(CELLS, CELLS + count),)], value)
    return value


def mix_group(base, count, halo_on, got, halo, tw_ref, tmp):
    head = lax.axis_index("head")
    place = lax.broadcasted_iota(jnp.int32, (count, 128), 1)
    pending = [None] * FRAMES
    for owner in range(STRIPS):
        slot = head ^ owner
        for lane in range(2):
            acts = [jnp.where(halo_on, cells(halo, (slot, i), base, count, lane), 0.0) for i in range(2)]
            acts += [cells(got[f // 2], (slot, f % 2), base, count, lane) for f in range(FRAMES)]
            w = [tw_ref[owner, i:i + 1, 128 * lane:128 * lane + 128] for i in range(3)]
            width = 128 if lane == 0 else 96
            tile, shift = divmod(224 * owner + 128 * lane, 128)
            for f in range(FRAMES):
                val = w[0] * acts[f + 2] + w[1] * acts[f + 1] + w[2] * acts[f]
                full = val
                if shift:
                    val = pltpu.roll(val, shift, 1)
                    full = jnp.where(place < shift, pending[f], val)
                if shift + width >= 128:
                    tmp[tile, pl.ds(f, count, stride=4), :] = full
                    pending[f] = val
                else:
                    pending[f] = full


def mix_kernel(got_early, got_late, halo, tw_ref, gq, gk, gv, gq_out, gk_out, gv_out, mixed_out, tmp, tw, mixed, sem, msem):
    plain = [
        pltpu.make_async_copy(src, dst, sem.at[i])
        for i, (src, dst) in enumerate(((gq, gq_out), (gk, gk_out), (gv, gv_out)))
    ]
    for c in plain:
        c.start()
    for owner in range(STRIPS):
        begin = min(224 * owner, 1792 - 256)
        part = tw_ref[:, begin:begin + 256]
        if begin < 224 * owner:
            part = pltpu.roll(part, 256 - (224 * owner - begin), 1)
        tw[owner, 0:3] = part
    halo_on = lax.axis_index("seg") > 0

    def leaving(base, count, i):
        rows = pl.ds(base, count)
        return pltpu.make_async_copy(mixed.at[rows], mixed_out.at[rows], msem.at[i])

    def group(base, count, g):
        mix_group(base, count, halo_on, (got_late, got_early), halo, tw, tmp)
        for i in range(count):
            for t in range(14):
                mixed[base + i, :, 128 * t:128 * t + 128] = tmp[t, 4 * i:4 * i + 4, :]
        leaving(base, count, g).start()

    def step(i, carry):
        group(pl.multiple_of(8 * i, 8), 8, i)
        return carry

    lax.fori_loop(0, 9, step, 0)
    group(72, 8, 9)
    group(80, 8, 10)
    group(88, 8, 11)
    group(96, 4, 12)
    for g in range(13):
        leaving(8 * g, 4 if g == 12 else 8, g).wait()
    for c in plain:
        c.wait()


def mix(early, late, halo, tw, gq, gk, gv):
    vmem = pl.BlockSpec(memory_space=pltpu.VMEM)
    hbm = pl.BlockSpec(memory_space=pl.ANY)
    wide = jax.ShapeDtypeStruct(gq.shape, F32)
    return pl.pallas_call(
        mix_kernel,
        out_shape=(wide, wide, wide, jax.ShapeDtypeStruct((CELLS, FRAMES, 1792), F32)),
        in_specs=[vmem] * 7,
        out_specs=(hbm, hbm, hbm, hbm),
        scratch_shapes=[
            pltpu.VMEM((14, 32, 128), F32),
            pltpu.VMEM((STRIPS, 8, 256), F32),
            pltpu.VMEM((CELLS, FRAMES, 1792), F32),
            pltpu.SemaphoreType.DMA((3,)),
            pltpu.SemaphoreType.DMA((13,)),
        ],
        compiler_params=pltpu.CompilerParams(vmem_limit_bytes=MIX_LIMIT),
        name="mix",
    )(early, late, halo, tw, gq, gk, gv)


def body(query_feat, key_feat, value_feat, grad_out, spatial_weight, temporal_weight):
    gq, gk, gv, early, late, halo = main_call(query_feat, key_feat, value_feat, grad_out, spatial_weight)
    gq, gk, gv, mixed = mix(early, late, halo, temporal_weight, gq, gk, gv)
    mixed = jnp.transpose(mixed.reshape(ROWS, 5, FRAMES, STRIPS * HEADS * D), (2, 0, 1, 3))
    return gq, gk, gv, mixed


def solution(mesh):
    wide = P("head", "seg")
    in_specs = (wide, wide, wide, wide, P(), P())
    out_specs = (wide, wide, wide, P("seg", None, "head", None))
    return jax.shard_map(body, mesh=mesh, in_specs=in_specs, out_specs=out_specs, check_vma=False)
```
